256 devices in a mesh: gx: 8 (over y, core), gy: 32 (over x, z).
Axes of the slice: x: 4, y: 4, z: 8, core: 2. Of those that a mesh axis runs over, the one named last changes fastest.
Arguments:
- right_side: float32 [128, 1024, 128], P('gx', 'gy'), may hold values from -6 to 6
- first_guess: float32 [128, 1024, 128], P('gx', 'gy'), may hold values from -6 to 6
- recycled: bfloat16 [8, 128, 1024, 128], P(None, 'gx', 'gy'), may hold values from -4 to 4
- heights: int32 [128, 1024], P('gx', 'gy'), may hold values from 0 to 64, as said below
- ground_codes: int32 [128, 1024], P('gx', 'gy'), may hold values from 0 to 2
Outputs:
- solution: float32 [128, 1024, 128], P('gx', 'gy')
- residual: float32 [128, 1024, 128], P('gx', 'gy')
The draws below stay inside these ranges and needn't reach their ends.
Inputs may be any that keep to these rules, and one draw needn't show every extreme that they name: `heights`: height of the buildings standing in each column, 0 for open ground.
All inputs are finite; a program needn't handle non-finite values.
Results may differ from the reference program's by a relative error of at most 0.0003.
Values sent between devices are 32-bit elements; how exact they have to be, the bound alone decides.
No kernel may reach another device: no remote copies, remote signals or barrier semaphores. Data moves between devices by JAX's collectives and lax.ppermute only.
A program may use at most 64 MiB of HBM per device.

```python
import jax
import jax.numpy as jnp
from jax import lax

NZ = 128
RECYCLE = 8
OUTER = 2
SWEEPS = 3
NX = 128
NY = 1024


def basis_fields(key):
    noise = jax.random.normal(jax.random.fold_in(key, 31), (RECYCLE, NX, NY, NZ), jnp.float32)
    return jnp.clip(1.5 * noise, -4.0, 4.0)


def draw_recycled(key, part):
    return basis_fields(key).astype(jnp.bfloat16)


def draw_right_side(key, part):
    rough = jnp.clip(jax.random.normal(jax.random.fold_in(key, 5), (NX, NY, NZ), jnp.float32), -6.0, 6.0)
    sizes_key = jax.random.fold_in(key, 43)
    signs_key = jax.random.fold_in(key, 47)
    magnitude = jax.random.uniform(sizes_key, (RECYCLE,), jnp.float32, 0.25, 0.6)
    signs = jnp.where(jax.random.bernoulli(signs_key, 0.5, (RECYCLE,)), 1.0, -1.0)
    weights = magnitude * signs
    mixture = jnp.tensordot(weights, basis_fields(key), axes=1)
    return jnp.clip(rough + mixture, -6.0, 6.0)


def draw_heights(key, part):
    first_key, second_key = jax.random.split(jax.random.fold_in(key, 17))
    tall = jax.random.randint(first_key, (NX, NY), 1, NZ // 2 + 1)
    open_ground = jax.random.randint(second_key, (NX, NY), 0, 3) == 0
    result = jnp.where(open_ground, 0, tall).astype(jnp.int32)
    result = result.at[0, 0].set(NZ // 2)
    result = result.at[0, 1].set(0)
    return result


def touch_ends(values, own_key, smallest, top_value):
    longest = values.shape.index(max(values.shape))
    spots = []
    for shift in (0, 1):
        where = [jax.random.randint(jax.random.fold_in(own_key, axis), (), 0, length) for axis, length in enumerate(values.shape)]
        where[longest] = (where[longest] + shift) % values.shape[longest]
        spots.append(tuple(where))
    return values.at[spots[0]].set(smallest).at[spots[1]].set(top_value)


def level_of(key, extent, cuts, smallest, largest):
    gain, own = 1.0, jax.random.fold_in(key, 6)
    for position, blocks in cuts:
        steps = jnp.exp(jax.random.uniform(jax.random.fold_in(own, position), (blocks,), jnp.float32, smallest / len(cuts), largest / len(cuts)))
        gain = gain * jnp.repeat(steps, extent[position] // blocks).reshape([-1 if axis == position else 1 for axis in range(len(extent))])
    return gain


def normal_values(key, dims, width, reach, cuts=(), dtype=jnp.bfloat16):
    values = jax.random.normal(key, dims, jnp.float32) * width
    if len(cuts) > 0:
        values = level_of(key, dims, cuts, -0.22, 0.18) * values
    return jnp.clip(values, min=-reach, max=reach).astype(dtype)


def setup_inputs(seed: int = 0) -> dict:
    keys = jax.random.split(jax.random.key(seed), 6)
    return {
        "right_side": draw_right_side(jax.random.fold_in(keys[5], 71), 0),
        "first_guess": normal_values(keys[1], (NX, NY, NZ), 1.0, 6.0, ((0, 8), (1, 32)), jnp.float32),
        "recycled": draw_recycled(jax.random.fold_in(keys[5], 71), 0),
        "heights": draw_heights(jax.random.fold_in(keys[5], 71), 0),
        "ground_codes": touch_ends(jax.random.randint(keys[4], (NX, NY), 0, 3), jax.random.fold_in(keys[4], 1), 0, 2).astype(jnp.int32),
    }


cheb_center = 7.25
cheb_half = 6.75
cheb_sigma = 7.25 / 6.75

def coefficients(ground):
    level = lax.broadcasted_iota(jnp.int32, (1, 1, NZ), 2)
    height = ground[0][:, :, None]
    code_col = ground[1][:, :, None]
    inside = ground[2][:, :, None]
    fluid_mask = jnp.where((inside > 0) & (level >= height), 1.0, 0.0).astype(jnp.float32)
    bottom = jnp.where(code_col == 1, 0.5, 0.0) + jnp.where(code_col == 2, 2.0, 0.0)
    extra_diag = jnp.where(level == 0, bottom, 0.0) + jnp.where(level == NZ - 1, 1.0, 0.0)
    return (fluid_mask, extra_diag.astype(jnp.float32))

def shift_upper(arr):
    return jnp.concatenate([arr[..., 1:], jnp.zeros_like(arr[..., :1])], -1)

def shift_lower(arr):
    return jnp.concatenate([jnp.zeros_like(arr[..., :1]), arr[..., :-1]], -1)

def operate(field_wide, fluid_mask, extra_diag):
    rows_a = fluid_mask.shape[0] - 2
    rows_b = fluid_mask.shape[1] - 2
    center_fluid = fluid_mask[1:-1, 1:-1]
    center_extra = extra_diag[1:-1, 1:-1]
    center_value = field_wide[..., 1:-1, 1:-1, :]
    summed = jnp.zeros_like(center_value)
    for off_a, off_b in ((2, 1), (0, 1), (1, 2), (1, 0)):
        near_fluid = fluid_mask[off_a:off_a + rows_a, off_b:off_b + rows_b]
        near_value = field_wide[..., off_a:off_a + rows_a, off_b:off_b + rows_b, :]
        summed = summed + near_fluid * (center_value - near_value)
    summed = summed + shift_upper(center_fluid) * (center_value - shift_upper(center_value))
    summed = summed + shift_lower(center_fluid) * (center_value - shift_lower(center_value))
    return center_fluid * (summed + center_extra * center_value) + (1.0 - center_fluid) * center_value

def padded_rim(field):
    return jnp.pad(field, ((1, 1), (1, 1), (0, 0)))

def small_solve(factor, vector):
    inner = lax.linalg.triangular_solve(factor, vector[:, None], left_side=True, lower=True)
    outer = lax.linalg.triangular_solve(factor, inner, left_side=True, lower=True, transpose_a=True)
    return outer[:, 0]

def project(vectors, field):
    return jnp.einsum('kxyz,xyz->k', vectors, field, precision=lax.Precision.HIGHEST)

def combine(coeffs, vectors):

    def add_one(carry, pair):
        return (carry + pair[0] * pair[1].astype(jnp.float32), None)
    result, unused = lax.scan(add_one, jnp.zeros(vectors.shape[1:], jnp.float32), (coeffs, vectors))
    return result

def reference(right_side, first_guess, recycled, heights, ground_codes):
    ground = jnp.stack([heights, ground_codes, jnp.ones_like(heights)], 0)
    ground = jnp.pad(ground, ((0, 0), (1, 1), (1, 1)))
    fluid_mask, extra_diag = coefficients(ground)
    images = lax.map(lambda vector: operate(padded_rim(vector.astype(jnp.float32)), fluid_mask, extra_diag), recycled)
    residual = right_side - operate(padded_rim(first_guess), fluid_mask, extra_diag)
    gram_matrix = jnp.einsum('kxyz,jxyz->kj', images, images, precision=lax.Precision.HIGHEST)
    start_proj = project(images, residual)
    factor = jnp.linalg.cholesky(gram_matrix)
    coeffs = small_solve(factor, start_proj)
    solution = first_guess + combine(coeffs, recycled)
    residual = residual - combine(coeffs, images)
    for outer_index in range(OUTER):
        correction = jnp.zeros_like(residual)
        remainder = residual
        direction = residual / cheb_center
        ratio_now = 1.0 / cheb_sigma
        for sweep_index in range(SWEEPS):
            correction = correction + direction
            remainder = remainder - operate(padded_rim(direction), fluid_mask, extra_diag)
            if sweep_index + 1 < SWEEPS:
                ratio_next = 1.0 / (2.0 * cheb_sigma - ratio_now)
                direction = ratio_next * ratio_now * direction + 2.0 * ratio_next / cheb_half * remainder
                ratio_now = ratio_next
        image_step = residual - remainder
        coeffs = small_solve(factor, project(images, image_step))
        image_step = image_step - combine(coeffs, images)
        correction = correction - combine(coeffs, recycled)
        step_length = jnp.sum(image_step * residual) / jnp.sum(image_step * image_step)
        solution = solution + step_length * correction
        residual = residual - step_length * image_step
    return (solution, residual)
```

```python
import jax
import jax.numpy as jnp
from jax import lax
from jax.experimental import pallas as pl
from jax.experimental.pallas import tpu as pltpu
from jax.sharding import PartitionSpec as P

NZ = 128
K = 8
H = 7
NA = 16
NB = 32
PA = NA + 2 * H
PB = NB + 2 * H
QB = NB + 16

CENTER = 7.25
HALF = 6.75
SIGMA = CENTER / HALF
T3 = 4.0 * SIGMA**3 - 3.0 * SIGMA
E3 = 1.0 / T3
TWO = 2.0 / HALF
SOLID = (CENTER - 1.0) / HALF
TS = [1.0, SOLID]
for _ in range(5):
    TS.append(2.0 * SOLID * TS[-1] - TS[-2])
P0 = (4.0 * SIGMA**2 - 1.0) / (HALF * T3)
P1 = 4.0 * SIGMA / (HALF * T3)
P2 = 2.0 / (HALF * T3)

XR, XG, XS, XN = 0, 224, 252, 280
XTILES = 282
YR, YG, YS, YN = 0, 112, 128, 144
YTILES = 148
TRI = [(d, e) for d in range(1, H) for e in range(1, H + 1 - d)]
CG, CS, CN = len(TRI), len(TRI) + 7, len(TRI) + 14
CHALF = len(TRI) + 16
CTILES = 2 * CHALF

f32 = jnp.float32
VMEM = pl.BlockSpec(memory_space=pltpu.VMEM)


def pack_kernel(rec, guess, right, heights, codes, rm, gnd, sxp, sxm, syp, sym):
    for m in range(K):

        def body(a, carry, m=m):
            rm[pl.ds(a * (NB * K) + m, NB, stride=K), :] = rec[m, a].astype(f32)
            return carry

        lax.fori_loop(0, NA, body, 0)
    for t in range(4):
        gnd[t] = jnp.zeros((8, 128), f32)
    for t in range(2):
        gnd[t, :, 0:NB] = (NZ - heights[8 * t : 8 * t + 8, :]).astype(f32)
        gnd[2 + t, :, 0:NB] = codes[8 * t : 8 * t + 8, :].astype(f32)
    for out, lo in ((sxp, NA - H), (sxm, 0)):
        for i in range(H):
            a = lo + i
            for b in range(NB):
                out[XR + i * NB + b] = rm[(a * NB + b) * K : (a * NB + b + 1) * K, :]
            for t in range(4):
                out[XG + i * 4 + t] = guess[a, 8 * t : 8 * t + 8, :]
                out[XS + i * 4 + t] = right[a, 8 * t : 8 * t + 8, :]
        for t in range(2):
            out[XN + t] = jnp.zeros((8, 128), f32)
        out[XN, 0:H, 0:NB] = (NZ - heights[lo : lo + H, :]).astype(f32)
        out[XN + 1, 0:H, 0:NB] = codes[lo : lo + H, :].astype(f32)
    for out, lo, tile in ((syp, NB - H, 3), (sym, 0, 0)):
        for a in range(NA):
            for i in range(H):
                b = lo + i
                out[YR + a * H + i] = rm[(a * NB + b) * K : (a * NB + b + 1) * K, :]
            out[YG + a] = guess[a, 8 * tile : 8 * tile + 8, :]
            out[YS + a] = right[a, 8 * tile : 8 * tile + 8, :]
        for t in range(4):
            out[YN + t] = gnd[t]


def corner_row(side, d):
    return H - d if side == 0 else d - 1


def corner_kernel(fxm, fxp, cp, cm):
    for out, high in ((cp, True), (cm, False)):
        for side, src in ((0, fxm), (1, fxp)):
            base = side * CHALF
            for n, (d, e) in enumerate(TRI):
                b = NB - e if high else e - 1
                out[base + n] = src[XR + corner_row(side, d) * NB + b]
            tile = 3 if high else 0
            for i in range(H):
                out[base + CG + i] = src[XG + i * 4 + tile]
                out[base + CS + i] = src[XS + i * 4 + tile]
            out[base + CN] = src[XN]
            out[base + CN + 1] = src[XN + 1]


def main_kernel(
    rm, guess, right, gnd, fxm, fxp, fym, fyp, cym, cyp,
    pay, tm, tr, rs, fo,
    ua, ub, em, fm, en, fn, va, vb, gs, gt,
):
    lane = lax.broadcasted_iota(jnp.int32, (8, 128), 1)
    sub = lax.broadcasted_iota(jnp.int32, (8, 128), 0)
    lane48 = lax.broadcasted_iota(jnp.int32, (QB, 128), 1)
    low8, high8 = lane > 0, lane < NZ - 1
    low48, high48 = lane48 > 0, lane48 < NZ - 1

    def widen(mid, left, right_):
        out = jnp.where((lane >= 8) & (lane < 40), pltpu.roll(mid, 8, 1), 0.0)
        out = jnp.where(lane < 8, pltpu.roll(left, 104, 1), out)
        return jnp.where((lane >= 40) & (lane < 48), pltpu.roll(right_, 40, 1), out)

    for q in range(2):
        gs[q] = jnp.zeros((128, 128), f32)
        gs[q, 0:8, :] = widen(fxm[XN + q], cym[CN + q], cyp[CN + q])
        for t in range(2):
            mid = widen(gnd[2 * q + t], fym[YN + 2 * q + t], fyp[YN + 2 * q + t])
            gs[q, H + 8 * t : H + 8 * t + 8, :] = mid
        last = widen(fxp[XN + q], cym[CHALF + CN + q], cyp[CHALF + CN + q])
        gs[q, H + NA : H + NA + 8, :] = last
        gt[q] = gs[q].T
    for a in range(PA):
        g = jnp.broadcast_to(gt[0, 0:QB, a : a + 1], (QB, 128))
        c = jnp.broadcast_to(gt[1, 0:QB, a : a + 1], (QB, 128))
        fluid = jnp.where(lane48.astype(f32) >= NZ - g, 1.0, 0.0)
        fn[a] = fluid
        bottom = jnp.where(c == 1.0, 0.5, jnp.where(c == 2.0, 2.0, 0.0))
        en[a] = jnp.where(low48, 0.0, bottom) + jnp.where(high48, 0.0, 1.0)

    def around(ref, a, c):
        s = ref[a - 1] + ref[a + 1]
        s = s + pltpu.roll(c, 1, 0) + pltpu.roll(c, QB - 1, 0)
        s = s + jnp.where(low48, pltpu.roll(c, 1, 1), 0.0)
        return s + jnp.where(high48, pltpu.roll(c, NZ - 1, 1), 0.0)

    def spread(a):
        f = fn[a] * TWO
        for b in range(PB):
            fm[a, b] = jnp.broadcast_to(f[b + 1 : b + 2, :], (8, 128))

    def coefficients(a, carry):
        diag = around(fn, a, fn[a]) + en[a]
        e = (CENTER - diag) * TWO
        en[a] = e
        for b in range(PB):
            em[a, b] = jnp.broadcast_to(e[b + 1 : b + 2, :], (8, 128))
        spread(a)
        return carry

    lax.fori_loop(1, PA - 1, coefficients, 0)
    spread(0)
    spread(PA - 1)

    def keep(a, b, value):
        ua[a, b] = jnp.where(fm[a, b] > 0.0, value, 0.0)

    zero8 = jnp.zeros((8, 128), f32)
    for i in range(H):
        for b in range(H):
            for a in (i, H + NA + i):
                ua[a, b] = zero8
                ua[a, H + NB + b] = zero8
    for side, src in ((0, fxm), (1, fxp)):
        top = 0 if side == 0 else H + NA
        def rows(i, carry, src=src, top=top):
            for b in range(NB):
                keep(top + i, H + b, src[XR + i * NB + b])
            return carry
        lax.fori_loop(0, H, rows, 0)
        for n, (d, e) in enumerate(TRI):
            a = top + corner_row(side, d)
            keep(a, H - e, cym[side * CHALF + n])
            keep(a, H + NB + e - 1, cyp[side * CHALF + n])

    def own(a, carry):
        for b in range(NB):
            keep(H + a, H + b, rm[a, b])
        for i in range(H):
            keep(H + a, i, fym[YR + a * H + i])
            keep(H + a, H + NB + i, fyp[YR + a * H + i])
        return carry

    lax.fori_loop(0, NA, own, 0)

    for ref, mid, xo, yo, co in ((va, guess, XG, YG, CG), (vb, right, XS, YS, CS)):
        for a in range(NA):
            ref[H + a, 8:40, :] = mid[a]
            ref[H + a, 0:8, :] = fym[yo + a]
            ref[H + a, 40:48, :] = fyp[yo + a]
        for side, src in ((0, fxm), (1, fxp)):
            top = 0 if side == 0 else H + NA
            for i in range(H):
                for t in range(4):
                    ref[top + i, 8 + 8 * t : 16 + 8 * t, :] = src[xo + 4 * i + t]
                ref[top + i, 0:8, :] = cym[side * CHALF + co + i]
                ref[top + i, 40:48, :] = cyp[side * CHALF + co + i]
    for a in range(NA):
        f = fn[H + a, 8:40, :]
        fo[a] = f
        rs[a] = jnp.where(f > 0.0, 0.0, right[a] - guess[a])
    for a in range(PA):
        wet = fn[a] > 0.0
        va[a] = jnp.where(wet, va[a], 0.0)
        vb[a] = jnp.where(wet, vb[a], 0.0)

    def doubled_row(ref, a):
        c = ref[a]
        return c, en[a] * c + fn[a] * TWO * around(ref, a, c)

    def sweep(src, dst, vsrc, vdst, halo, level):
        lo_a, hi_a = H - halo, H + NA + halo
        lo_b, hi_b = H - halo, H + NB + halo

        def step(a, inner):
            before, here = src[a, lo_b - 1], src[a, lo_b]
            for b in range(lo_b, hi_b):
                after = src[a, b + 1]
                s = (src[a - 1, b] + src[a + 1, b]) + (before + after)
                s = s + jnp.where(low8, pltpu.roll(here, 1, 1), 0.0)
                s = s + jnp.where(high8, pltpu.roll(here, NZ - 1, 1), 0.0)
                two = em[a, b] * here + fm[a, b] * s
                if level == 0:
                    out = CENTER * here - (0.5 * HALF) * two
                elif level == 1:
                    out = 0.5 * two
                else:
                    out = two - dst[a, b]
                dst[a, b] = out
                if inner and H <= b < H + NB:
                    tm[level, a - H, b - H] = out
                before, here = here, after
            c, two = doubled_row(vsrc, a)
            if level == 0:
                out = vdst[a] - (CENTER * c - (0.5 * HALF) * two)
            elif level == 1:
                out = 0.5 * two
            else:
                out = two - vdst[a]
            vdst[a] = out
            if inner:
                tr[level, a - H] = out[8:40, :]

        def outer_rows(a, carry):
            step(a, False)
            return carry

        def inner_rows(a, carry):
            step(a, True)
            return carry

        if halo:
            lax.fori_loop(lo_a, H, outer_rows, 0)
        lax.fori_loop(H, H + NA, inner_rows, 0)
        if halo:
            lax.fori_loop(H + NA, hi_a, outer_rows, 0)

    for level in range(7):
        if level % 2 == 0:
            sweep(ua, ub, va, vb, 6 - level, level)
        else:
            sweep(ub, ua, vb, va, 6 - level, level)

    def products(acc, left, right_):
        out = []
        for k in range(5):
            turned = left if k == 0 else pltpu.roll(left, k, 0)
            out.append(acc[k] + right_ * turned)
        return out

    def row(tile, q):
        return jnp.broadcast_to(tile[q : q + 1, :], (8, 128))

    def first(i, carry):
        g00, g03, gss, b0, b3, bs, p0, p3, ps = carry
        a, t = i // 4, i % 4
        r0 = tr[0, a, pl.ds(t * 8, 8), :]
        r3 = tr[3, a, pl.ds(t * 8, 8), :]
        rr = rs[a, pl.ds(t * 8, 8), :]
        ff = fo[a, pl.ds(t * 8, 8), :]
        p0, p3, ps = p0 + r0 * r0, p3 + r0 * r3, ps + rr * rr
        for q in range(8):
            u0, u3 = tm[0, a, t * 8 + q], tm[3, a, t * 8 + q]
            us = jnp.where(row(ff, q) > 0.0, 0.0, rm[a, t * 8 + q])
            turned = [u0] + [pltpu.roll(u0, k, 0) for k in range(1, 5)]
            g00 = [g + u0 * v for g, v in zip(g00, turned)]
            g03 = [g + u3 * v for g, v in zip(g03, turned)]
            gss = products(gss, us, us)
            b0 = b0 + u0 * row(r0, q)
            b3 = b3 + u0 * row(r3, q)
            bs = bs + us * row(rr, q)
        return g00, g03, gss, b0, b3, bs, p0, p3, ps

    def second(i, carry):
        g33, g36, g66, b33, b36, b66, p33, p36, p66 = carry
        a, t = i // 4, i % 4
        r3 = tr[3, a, pl.ds(t * 8, 8), :]
        r6 = tr[6, a, pl.ds(t * 8, 8), :] + tr[0, a, pl.ds(t * 8, 8), :]
        p33, p36, p66 = p33 + r3 * r3, p36 + r3 * r6, p66 + r6 * r6
        for q in range(8):
            u3 = tm[3, a, t * 8 + q]
            u6 = tm[6, a, t * 8 + q] + tm[0, a, t * 8 + q]
            turned = [u3] + [pltpu.roll(u3, k, 0) for k in range(1, 5)]
            g33 = [g + u3 * v for g, v in zip(g33, turned)]
            g36 = [g + u6 * v for g, v in zip(g36, turned)]
            g66 = products(g66, u6, u6)
            b33 = b33 + u3 * row(r3, q)
            b36 = b36 + u3 * row(r6, q)
            b66 = b66 + u6 * row(r6, q)
        return g33, g36, g66, b33, b36, b66, p33, p36, p66

    five = [zero8] * 5
    start = (five, five, five, zero8, zero8, zero8, zero8, zero8, zero8)
    g00, g03, gss, b0, b3, bs, p0, p3, ps = lax.fori_loop(0, NA * 4, first, start)
    g33, g36, g66, b33, b36, b66, p33, p36, p66 = lax.fori_loop(0, NA * 4, second, start)
    wet = (1.0, E3, E3**2, 0.5 * E3**3, 0.25 * E3**4)
    dry = [(E3 * TS[3]) ** k for k in range(5)]
    packed = zero8
    for k, (g, b, p) in enumerate(
        ((g00, b0, p0), (g03, b3, p3), (g33, b33, p33), (g36, b36, p36), (g66, b66, p66))
    ):
        for r in range(5):
            value = jnp.sum(wet[k] * g[r] + dry[k] * gss[r], axis=1, keepdims=True)
            packed = jnp.where(lane == 5 * k + r, value, packed)
        value = jnp.sum(wet[k] * b + dry[k] * bs, axis=1, keepdims=True)
        packed = jnp.where(lane == 25 + k, value, packed)
        value = jnp.sum(wet[k] * p + dry[k] * ps, axis=1, keepdims=True)
        value = jnp.sum(value, axis=0, keepdims=True)
        packed = jnp.where((lane == 30) & (sub == k), value, packed)
    packed = jnp.where(lane < 32, packed, 0.0)
    quarter = sub % 4
    moved = packed
    for i in range(1, 4):
        moved = jnp.where(quarter == i, pltpu.roll(packed, 32 * i, 1), moved)
    upper = jnp.sum(jnp.where(sub < 4, moved, 0.0), axis=0, keepdims=True)
    lower = jnp.sum(jnp.where(sub < 4, 0.0, moved), axis=0, keepdims=True)
    both = jnp.concatenate([upper, lower], axis=0)
    pay[...] = jnp.broadcast_to(both[None], pay.shape)


def tail_kernel(got, rm, guess, tm, tr, rs, fo, out_x, out_r):
    lane = lax.broadcasted_iota(jnp.int32, (8, 128), 1)
    sub = lax.broadcasted_iota(jnp.int32, (8, 128), 0)
    total = jnp.sum(got[...], axis=0)
    spread = jnp.where(
        sub < 4,
        jnp.broadcast_to(total[0:1, :], (8, 128)),
        jnp.broadcast_to(total[1:2, :], (8, 128)),
    )
    quarter = sub % 4
    packed = spread
    for i in range(1, 4):
        packed = jnp.where(quarter == i, pltpu.roll(spread, 128 - 32 * i, 1), packed)

    def column(j):
        return jnp.broadcast_to(packed[:, j : j + 1], (8, 128))

    def over_m(v):
        return jnp.broadcast_to(jnp.sum(v, axis=0, keepdims=True), (8, 128))

    diag = [[column(5 * k + r) for r in range(5)] for k in range(5)]
    cross = [column(25 + k) for k in range(5)]
    powers = column(30)
    rho = [over_m(jnp.where(sub == k, powers, 0.0)) for k in range(5)]

    def times(k, v):
        out = diag[k][0] * v
        for r in range(1, 5):
            out = out + diag[k][r] * pltpu.roll(v, r, 0)
        for r in range(1, 4):
            out = out + pltpu.roll(diag[k][r] * v, 8 - r, 0)
        return out

    mat = jnp.where(lane == sub + 8, 1.0, 0.0)
    for r in range(5):
        mat = jnp.where(lane == (sub + 8 - r) % 8, diag[0][r], mat)
    for r in range(1, 4):
        mat = jnp.where(lane == (sub + r) % 8, pltpu.roll(diag[0][r], 8 - r, 0), mat)
    for k in range(8):
        pivot_row = jnp.broadcast_to(mat[k : k + 1, :], (8, 128))
        pivot_row = pivot_row / jnp.broadcast_to(pivot_row[:, k : k + 1], (8, 128))
        factor = jnp.broadcast_to(mat[:, k : k + 1], (8, 128))
        mat = jnp.where(sub == k, pivot_row, mat - factor * pivot_row)
    inverse = jnp.where((lane >= 8) & (lane < 16), mat, 0.0)

    def solve(v):
        flat = over_m(jnp.where(lane == sub + 8, v, 0.0))
        return jnp.broadcast_to(
            jnp.sum(inverse * flat, axis=1, keepdims=True), (8, 128)
        )

    def apply(k, v):
        return times(k, v[0]) + cross[k] * v[1], over_m(cross[k] * v[0]) + rho[k] * v[1]

    def dot(u, v):
        return over_m(u[0] * v[0]) + u[1] * v[1]

    coeffs = solve(cross[0])
    one = jnp.ones((8, 128), f32)
    a = (-coeffs, one)
    n0, n1, n2 = apply(0, a), apply(1, a), apply(2, a)
    g = n0[0] - n1[0]
    y1 = solve(g)
    rr, re, ee = dot(a, n0), dot(a, n1), dot(a, n2)
    s1 = (rr - re - over_m(y1 * n0[0])) / (rr - 2.0 * re + ee - over_m(y1 * g))
    a0 = ((1.0 - s1) * a[0] + s1 * y1, (1.0 - s1) * a[1])
    a1 = (s1 * a[0], s1 * a[1])
    m0, m1, m2, m3 = apply(0, a0), apply(1, a0), apply(2, a0), apply(3, a0)
    l3, l4 = apply(3, a1), apply(4, a1)
    h = m0[0] + s1 * n1[0]
    g = h - (m1[0] + s1 * n2[0])
    y2 = solve(g)
    rr = dot(a0, m0) + 2.0 * dot(a1, m1) + s1 * dot(a1, n2)
    re = dot(a0, m1) + 2.0 * dot(a1, m2) + dot(a1, l3)
    ee = dot(a0, m2) + 2.0 * dot(a1, m3) + dot(a1, l4)
    s2 = (rr - re - over_m(y2 * h)) / (rr - 2.0 * re + ee - over_m(y2 * g))

    half = 0.5 * E3 * E3
    weights_r, weights_x = [], []
    for i in range(2):
        extra = s2 * y2 if i == 0 else 0.0
        weights_r.append((
            (1.0 - s2) * a0[i] + extra + half * s2 * a1[i],
            E3 * ((1.0 - s2) * a1[i] + s2 * a0[i]),
            half * s2 * a1[i],
        ))
        d0 = s1 * a[i] + s2 * a0[i]
        d1 = E3 * s2 * a1[i]
        weights_x.append((
            P0 * d0,
            P1 * d0 + (0.5 * P2) * d1,
            P2 * d0 + (0.5 * P1) * d1,
            P0 * d1,
            (0.5 * P1) * d1,
            (0.5 * P2) * d1,
        ))
    direct = coeffs - s1 * y1 - s2 * y2
    levels_r = (0, 3, 6)
    solid_r = [sum(w * TS[j] for w, j in zip(ws, levels_r)) for ws in weights_r]
    solid_x = [sum(w * TS[j] for j, w in enumerate(ws)) for ws in weights_x]

    def tile(i, carry):
        p, t = i // 4, i % 4
        rows = pl.ds(t * 8, 8)
        ff = fo[p, rows, :]
        base_x = guess[p, rows, :]
        base_r = jnp.zeros((8, 128), f32)
        for q in range(8):
            b = t * 8 + q
            r = rm[p, b]
            dry = jnp.where(jnp.broadcast_to(ff[q : q + 1, :], (8, 128)) > 0.0, 0.0, r)
            us = [tm[j, p, b] for j in range(7)]
            vx = direct * r + solid_x[0] * dry
            for j in range(6):
                vx = vx + weights_x[0][j] * us[j]
            vr = solid_r[0] * dry
            for w, j in zip(weights_r[0], levels_r):
                vr = vr + w * us[j]
            base_x = jnp.where(sub == q, base_x + over_m(vx), base_x)
            base_r = jnp.where(sub == q, base_r + over_m(vr), base_r)
        dry = rs[p, rows, :]
        vs = [tr[j, p, rows, :] for j in range(7)]
        base_x = base_x + solid_x[1] * dry
        base_r = base_r + solid_r[1] * dry
        for j in range(6):
            base_x = base_x + weights_x[1][j] * vs[j]
        for w, j in zip(weights_r[1], levels_r):
            base_r = base_r + w * vs[j]
        out_x[p, rows, :] = base_x
        out_r[p, rows, :] = base_r
        return carry

    lax.fori_loop(0, NA * 4, tile, 0)


def call(kernel, outs, scratch, limit, *args):
    return pl.pallas_call(
        kernel,
        out_shape=tuple(jax.ShapeDtypeStruct(s, f32) for s in outs),
        in_specs=[VMEM] * len(args),
        out_specs=tuple([VMEM] * len(outs)),
        scratch_shapes=[pltpu.VMEM(s, f32) for s in scratch],
        compiler_params=pltpu.CompilerParams(vmem_limit_bytes=limit),
    )(*args)


def local(right_side, first_guess, recycled, heights, ground_codes):
    mib = 1 << 20
    rm, gnd, sxp, sxm, syp, sym = call(
        pack_kernel,
        ((NA * NB * K, 128), (4, 8, 128), (XTILES, 8, 128), (XTILES, 8, 128),
         (YTILES, 8, 128), (YTILES, 8, 128)),
        (),
        16 * mib,
        recycled, first_guess, right_side, heights, ground_codes,
    )
    rm = rm.reshape(NA, NB, K, 128)

    def shift(value, axis, way):
        size = lax.axis_size(axis)
        pairs = [(i, i + way) for i in range(size) if 0 <= i + way < size]
        return lax.ppermute(value, axis, pairs)

    fxm, fxp = shift(sxp, "gx", 1), shift(sxm, "gx", -1)
    fym, fyp = shift(syp, "gy", 1), shift(sym, "gy", -1)
    cp, cm = call(
        corner_kernel, ((CTILES, 8, 128), (CTILES, 8, 128)), (), 16 * mib, fxm, fxp
    )
    cym, cyp = shift(cp, "gy", 1), shift(cm, "gy", -1)
    wide, flat = (PA, PB, 8, 128), (PA, QB, 128)
    pay, tm, tr, rs, fo = call(
        main_kernel,
        ((256, 2, 128), (7, NA, NB, 8, 128), (7, NA, NB, 128), (NA, NB, 128),
         (NA, NB, 128)),
        (wide, wide, wide, wide, flat, flat, flat, flat, (2, 128, 128), (2, 128, 128)),
        30 * mib,
        rm, first_guess, right_side, gnd, fxm, fxp, fym, fyp, cym, cyp,
    )
    got = lax.all_to_all(pay, ("gx", "gy"), 0, 0)
    return call(
        tail_kernel,
        ((NA, NB, 128), (NA, NB, 128)),
        (),
        8 * mib,
        got, rm, first_guess, tm, tr, rs, fo,
    )


def solution(mesh):
    placed = (
        P("gx", "gy", None),
        P("gx", "gy", None),
        P(None, "gx", "gy", None),
        P("gx", "gy"),
        P("gx", "gy"),
    )
    return jax.shard_map(
        local,
        mesh=mesh,
        in_specs=placed,
        out_specs=(P("gx", "gy", None), P("gx", "gy", None)),
        check_vma=False,
    )
```

```python
import jax
import jax.numpy as jnp
from jax import lax
from jax.experimental import pallas as pl
from jax.experimental.pallas import tpu as pltpu
from jax.sharding import PartitionSpec as P

NZ = 128
K = 8
H = 7
NA = 16
NB = 32
PA = NA + 2 * H
PB = NB + 2 * H
QB = NB + 16

CENTER = 7.25
HALF = 6.75
SIGMA = CENTER / HALF
T3 = 4.0 * SIGMA**3 - 3.0 * SIGMA
E3 = 1.0 / T3
TWO = 2.0 / HALF
SOLID = (CENTER - 1.0) / HALF
TS = [1.0, SOLID]
for _ in range(5):
    TS.append(2.0 * SOLID * TS[-1] - TS[-2])
P0 = (4.0 * SIGMA**2 - 1.0) / (HALF * T3)
P1 = 4.0 * SIGMA / (HALF * T3)
P2 = 2.0 / (HALF * T3)

XR, XG, XS, XN = 0, 224, 252, 280
XTILES = 282
YR, YG, YS, YN = 0, 112, 128, 144
YTILES = 148
TRI = [(d, e) for d in range(1, H) for e in range(1, H + 1 - d)]
CG, CS, CN = len(TRI), len(TRI) + 7, len(TRI) + 14
CHALF = len(TRI) + 16
CTILES = 2 * CHALF

f32 = jnp.float32
VMEM = pl.BlockSpec(memory_space=pltpu.VMEM)


def pack_kernel(
    rec_in, guess_in, right_in, heights_in, codes_in,
    rm, gnd, sxp, sxm, syp, sym,
    rec, guess, right, heights, codes, sems,
):
    copies = [pltpu.make_async_copy(rec_in.at[m], rec.at[m], sems.at[m]) for m in range(K)]
    others = ((guess_in, guess), (right_in, right), (heights_in, heights), (codes_in, codes))
    copies += [
        pltpu.make_async_copy(src, dst, sems.at[K + n]) for n, (src, dst) in enumerate(others)
    ]
    for copy in copies:
        copy.start()
    for m in range(K):
        copies[m].wait()

        def body(a, carry, m=m):
            rm[pl.ds(a * (NB * K) + m, NB, stride=K), :] = rec[m, a].astype(f32)
            return carry

        lax.fori_loop(0, NA, body, 0)
    for copy in copies[K:]:
        copy.wait()
    for t in range(4):
        gnd[t] = jnp.zeros((8, 128), f32)
    for t in range(2):
        gnd[t, :, 0:NB] = (NZ - heights[8 * t : 8 * t + 8, :]).astype(f32)
        gnd[2 + t, :, 0:NB] = codes[8 * t : 8 * t + 8, :].astype(f32)
    for out, lo in ((sxp, NA - H), (sxm, 0)):
        for i in range(H):
            a = lo + i
            for b in range(NB):
                out[XR + i * NB + b] = rm[(a * NB + b) * K : (a * NB + b + 1) * K, :]
            for t in range(4):
                out[XG + i * 4 + t] = guess[a, 8 * t : 8 * t + 8, :]
                out[XS + i * 4 + t] = right[a, 8 * t : 8 * t + 8, :]
        for t in range(2):
            out[XN + t] = jnp.zeros((8, 128), f32)
        out[XN, 0:H, 0:NB] = (NZ - heights[lo : lo + H, :]).astype(f32)
        out[XN + 1, 0:H, 0:NB] = codes[lo : lo + H, :].astype(f32)
    for out, lo, tile in ((syp, NB - H, 3), (sym, 0, 0)):
        for a in range(NA):
            for i in range(H):
                b = lo + i
                out[YR + a * H + i] = rm[(a * NB + b) * K : (a * NB + b + 1) * K, :]
            out[YG + a] = guess[a, 8 * tile : 8 * tile + 8, :]
            out[YS + a] = right[a, 8 * tile : 8 * tile + 8, :]
        for t in range(4):
            out[YN + t] = gnd[t]


def corner_row(side, d):
    return H - d if side == 0 else d - 1


def corner_kernel(fxm, fxp, cp, cm):
    for out, high in ((cp, True), (cm, False)):
        for side, src in ((0, fxm), (1, fxp)):
            base = side * CHALF
            for n, (d, e) in enumerate(TRI):
                b = NB - e if high else e - 1
                out[base + n] = src[XR + corner_row(side, d) * NB + b]
            tile = 3 if high else 0
            for i in range(H):
                out[base + CG + i] = src[XG + i * 4 + tile]
                out[base + CS + i] = src[XS + i * 4 + tile]
            out[base + CN] = src[XN]
            out[base + CN + 1] = src[XN + 1]


def main_kernel(
    rm, guess, right, gnd, fxm, fxp, fym, fyp, cym, cyp,
    pay, tm, tr, rs, fo,
    ua, ub, em, fm, en, fn, va, vb, gs, gt,
):
    lane = lax.broadcasted_iota(jnp.int32, (8, 128), 1)
    sub = lax.broadcasted_iota(jnp.int32, (8, 128), 0)
    lane48 = lax.broadcasted_iota(jnp.int32, (QB, 128), 1)
    low8, high8 = lane > 0, lane < NZ - 1
    low48, high48 = lane48 > 0, lane48 < NZ - 1

    def widen(mid, left, right_):
        out = jnp.where((lane >= 8) & (lane < 40), pltpu.roll(mid, 8, 1), 0.0)
        out = jnp.where(lane < 8, pltpu.roll(left, 104, 1), out)
        return jnp.where((lane >= 40) & (lane < 48), pltpu.roll(right_, 40, 1), out)

    for q in range(2):
        gs[q] = jnp.zeros((128, 128), f32)
        gs[q, 0:8, :] = widen(fxm[XN + q], cym[CN + q], cyp[CN + q])
        for t in range(2):
            mid = widen(gnd[2 * q + t], fym[YN + 2 * q + t], fyp[YN + 2 * q + t])
            gs[q, H + 8 * t : H + 8 * t + 8, :] = mid
        last = widen(fxp[XN + q], cym[CHALF + CN + q], cyp[CHALF + CN + q])
        gs[q, H + NA : H + NA + 8, :] = last
        gt[q] = gs[q].T
    for a in range(PA):
        g = jnp.broadcast_to(gt[0, 0:QB, a : a + 1], (QB, 128))
        c = jnp.broadcast_to(gt[1, 0:QB, a : a + 1], (QB, 128))
        fluid = jnp.where(lane48.astype(f32) >= NZ - g, 1.0, 0.0)
        fn[a] = fluid
        bottom = jnp.where(c == 1.0, 0.5, jnp.where(c == 2.0, 2.0, 0.0))
        en[a] = jnp.where(low48, 0.0, bottom) + jnp.where(high48, 0.0, 1.0)

    def around(ref, a, c):
        s = ref[a - 1] + ref[a + 1]
        s = s + pltpu.roll(c, 1, 0) + pltpu.roll(c, QB - 1, 0)
        s = s + jnp.where(low48, pltpu.roll(c, 1, 1), 0.0)
        return s + jnp.where(high48, pltpu.roll(c, NZ - 1, 1), 0.0)

    def spread(a):
        f = fn[a] * TWO
        for b in range(PB):
            fm[a, b] = jnp.broadcast_to(f[b + 1 : b + 2, :], (8, 128))

    def coefficients(a, carry):
        diag = around(fn, a, fn[a]) + en[a]
        e = (CENTER - diag) * TWO
        en[a] = e
        for b in range(PB):
            em[a, b] = jnp.broadcast_to(e[b + 1 : b + 2, :], (8, 128))
        spread(a)
        return carry

    lax.fori_loop(1, PA - 1, coefficients, 0)
    spread(0)
    spread(PA - 1)

    def keep(a, b, value):
        ua[a, b] = jnp.where(fm[a, b] > 0.0, value, 0.0)

    zero8 = jnp.zeros((8, 128), f32)
    for i in range(H):
        for b in range(H):
            for a in (i, H + NA + i):
                ua[a, b] = zero8
                ua[a, H + NB + b] = zero8
    for side, src in ((0, fxm), (1, fxp)):
        top = 0 if side == 0 else H + NA
        def rows(i, carry, src=src, top=top):
            for b in range(NB):
                keep(top + i, H + b, src[XR + i * NB + b])
            return carry
        lax.fori_loop(0, H, rows, 0)
        for n, (d, e) in enumerate(TRI):
            a = top + corner_row(side, d)
            keep(a, H - e, cym[side * CHALF + n])
            keep(a, H + NB + e - 1, cyp[side * CHALF + n])

    def own(a, carry):
        for b in range(NB):
            keep(H + a, H + b, rm[a, b])
        for i in range(H):
            keep(H + a, i, fym[YR + a * H + i])
            keep(H + a, H + NB + i, fyp[YR + a * H + i])
        return carry

    lax.fori_loop(0, NA, own, 0)

    for ref, mid, xo, yo, co in ((va, guess, XG, YG, CG), (vb, right, XS, YS, CS)):
        for a in range(NA):
            ref[H + a, 8:40, :] = mid[a]
            ref[H + a, 0:8, :] = fym[yo + a]
            ref[H + a, 40:48, :] = fyp[yo + a]
        for side, src in ((0, fxm), (1, fxp)):
            top = 0 if side == 0 else H + NA
            for i in range(H):
                for t in range(4):
                    ref[top + i, 8 + 8 * t : 16 + 8 * t, :] = src[xo + 4 * i + t]
                ref[top + i, 0:8, :] = cym[side * CHALF + co + i]
                ref[top + i, 40:48, :] = cyp[side * CHALF + co + i]
    for a in range(NA):
        f = fn[H + a, 8:40, :]
        fo[a] = f
        rs[a] = jnp.where(f > 0.0, 0.0, right[a] - guess[a])
    for a in range(PA):
        wet = fn[a] > 0.0
        va[a] = jnp.where(wet, va[a], 0.0)
        vb[a] = jnp.where(wet, vb[a], 0.0)

    def doubled_row(ref, a):
        c = ref[a]
        return c, en[a] * c + fn[a] * TWO * around(ref, a, c)

    def sweep(src, dst, vsrc, vdst, halo, level):
        lo_a, hi_a = H - halo, H + NA + halo
        lo_b, hi_b = H - halo, H + NB + halo

        def step(a, inner):
            before, here = src[a, lo_b - 1], src[a, lo_b]
            for b in range(lo_b, hi_b):
                after = src[a, b + 1]
                s = (src[a - 1, b] + src[a + 1, b]) + (before + after)
                s = s + jnp.where(low8, pltpu.roll(here, 1, 1), 0.0)
                s = s + jnp.where(high8, pltpu.roll(here, NZ - 1, 1), 0.0)
                two = em[a, b] * here + fm[a, b] * s
                if level == 0:
                    out = CENTER * here - (0.5 * HALF) * two
                elif level == 1:
                    out = 0.5 * two
                else:
                    out = two - dst[a, b]
                dst[a, b] = out
                if inner and H <= b < H + NB:
                    tm[level, a - H, b - H] = out
                before, here = here, after
            c, two = doubled_row(vsrc, a)
            if level == 0:
                out = vdst[a] - (CENTER * c - (0.5 * HALF) * two)
            elif level == 1:
                out = 0.5 * two
            else:
                out = two - vdst[a]
            vdst[a] = out
            if inner:
                tr[level, a - H] = out[8:40, :]

        def outer_rows(a, carry):
            step(a, False)
            return carry

        def inner_rows(a, carry):
            step(a, True)
            return carry

        if halo:
            lax.fori_loop(lo_a, H, outer_rows, 0)
        lax.fori_loop(H, H + NA, inner_rows, 0)
        if halo:
            lax.fori_loop(H + NA, hi_a, outer_rows, 0)

    for level in range(7):
        if level % 2 == 0:
            sweep(ua, ub, va, vb, 6 - level, level)
        else:
            sweep(ub, ua, vb, va, 6 - level, level)

    def row(tile, q):
        return jnp.broadcast_to(tile[q : q + 1, :], (8, 128))

    def joined(ref, at, dry):
        base = ref[(0, *at)]
        return (
            base + dry,
            ref[(3, *at)] + TS[3] * dry,
            (ref[(6, *at)] + base) + (TS[6] + 1.0) * dry,
        )

    def gather(i, carry):
        grams, cross, powers = carry
        a, t = i // 4, i % 4
        rows = pl.ds(t * 8, 8)
        r0, r3, r6 = joined(tr, (a, rows), rs[a, rows, :])
        pairs = (r0 * r0, r0 * r3, r0 * r6, r3 * r6, r6 * r6)
        powers = [p + v for p, v in zip(powers, pairs)]
        ff = fo[a, rows, :]
        for q in range(8):
            b = t * 8 + q
            dry = jnp.where(row(ff, q) > 0.0, 0.0, rm[a, b])
            t0, t3, t6 = joined(tm, (a, b), dry)
            new = [list(g) for g in grams]
            for k in range(5):
                v0 = t0 if k == 0 else pltpu.roll(t0, k, 0)
                v6 = t6 if k == 0 else pltpu.roll(t6, k, 0)
                for n, v in enumerate((t0 * v0, t3 * v0, t6 * v0, t3 * v6, t6 * v6)):
                    new[n][k] = new[n][k] + v
            grams = new
            w0, w3, w6 = row(r0, q), row(r3, q), row(r6, q)
            pairs = (t0 * w0, t0 * w3, t0 * w6, t3 * w6, t6 * w6)
            cross = [c + v for c, v in zip(cross, pairs)]
        return grams, cross, powers

    five = [zero8] * 5
    grams, cross, powers = lax.fori_loop(0, NA * 4, gather, ([five] * 5, five, five))
    scale = (1.0, E3, 0.5 * E3**2, 0.5 * E3**3, 0.25 * E3**4)
    packed = zero8
    for k in range(5):
        for r in range(5):
            value = scale[k] * jnp.sum(grams[k][r], axis=1, keepdims=True)
            packed = jnp.where(lane == 5 * k + r, value, packed)
        value = scale[k] * jnp.sum(cross[k], axis=1, keepdims=True)
        packed = jnp.where(lane == 25 + k, value, packed)
        value = scale[k] * jnp.sum(powers[k], axis=1, keepdims=True)
        value = jnp.sum(value, axis=0, keepdims=True)
        packed = jnp.where((lane == 30) & (sub == k), value, packed)
    packed = jnp.where(lane < 32, packed, 0.0)
    quarter = sub % 4
    moved = packed
    for i in range(1, 4):
        moved = jnp.where(quarter == i, pltpu.roll(packed, 32 * i, 1), moved)
    upper = jnp.sum(jnp.where(sub < 4, moved, 0.0), axis=0, keepdims=True)
    lower = jnp.sum(jnp.where(sub < 4, 0.0, moved), axis=0, keepdims=True)
    both = jnp.concatenate([upper, lower], axis=0)
    pay[...] = jnp.broadcast_to(both[None], pay.shape)


def tail_kernel(got, rm, guess, tm, tr, rs, fo, out_x, out_r):
    lane = lax.broadcasted_iota(jnp.int32, (8, 128), 1)
    sub = lax.broadcasted_iota(jnp.int32, (8, 128), 0)
    total = jnp.sum(got[...], axis=0)
    spread = jnp.where(
        sub < 4,
        jnp.broadcast_to(total[0:1, :], (8, 128)),
        jnp.broadcast_to(total[1:2, :], (8, 128)),
    )
    quarter = sub % 4
    packed = spread
    for i in range(1, 4):
        packed = jnp.where(quarter == i, pltpu.roll(spread, 128 - 32 * i, 1), packed)

    def column(j):
        return jnp.broadcast_to(packed[:, j : j + 1], (8, 128))

    def over_m(v):
        return jnp.broadcast_to(jnp.sum(v, axis=0, keepdims=True), (8, 128))

    diag = [[column(5 * k + r) for r in range(5)] for k in range(5)]
    cross = [column(25 + k) for k in range(5)]
    powers = column(30)
    rho = [over_m(jnp.where(sub == k, powers, 0.0)) for k in range(5)]

    def times(k, v):
        out = diag[k][0] * v
        for r in range(1, 5):
            out = out + diag[k][r] * pltpu.roll(v, r, 0)
        for r in range(1, 4):
            out = out + pltpu.roll(diag[k][r] * v, 8 - r, 0)
        return out

    mat = jnp.where(lane == sub + 8, 1.0, 0.0)
    for r in range(5):
        mat = jnp.where(lane == (sub + 8 - r) % 8, diag[0][r], mat)
    for r in range(1, 4):
        mat = jnp.where(lane == (sub + r) % 8, pltpu.roll(diag[0][r], 8 - r, 0), mat)
    for k in range(8):
        pivot_row = jnp.broadcast_to(mat[k : k + 1, :], (8, 128))
        pivot_row = pivot_row / jnp.broadcast_to(pivot_row[:, k : k + 1], (8, 128))
        factor = jnp.broadcast_to(mat[:, k : k + 1], (8, 128))
        mat = jnp.where(sub == k, pivot_row, mat - factor * pivot_row)
    inverse = jnp.where((lane >= 8) & (lane < 16), mat, 0.0)

    def solve(v):
        flat = over_m(jnp.where(lane == sub + 8, v, 0.0))
        return jnp.broadcast_to(
            jnp.sum(inverse * flat, axis=1, keepdims=True), (8, 128)
        )

    def apply(k, v):
        return times(k, v[0]) + cross[k] * v[1], over_m(cross[k] * v[0]) + rho[k] * v[1]

    def dot(u, v):
        return over_m(u[0] * v[0]) + u[1] * v[1]

    coeffs = solve(cross[0])
    one = jnp.ones((8, 128), f32)
    a = (-coeffs, one)
    n0, n1, n2 = apply(0, a), apply(1, a), apply(2, a)
    g = n0[0] - n1[0]
    y1 = solve(g)
    rr, re, ee = dot(a, n0), dot(a, n1), dot(a, n2)
    s1 = (rr - re - over_m(y1 * n0[0])) / (rr - 2.0 * re + ee - over_m(y1 * g))
    a0 = ((1.0 - s1) * a[0] + s1 * y1, (1.0 - s1) * a[1])
    a1 = (s1 * a[0], s1 * a[1])
    m0, m1, m2, m3 = apply(0, a0), apply(1, a0), apply(2, a0), apply(3, a0)
    l3, l4 = apply(3, a1), apply(4, a1)
    h = m0[0] + s1 * n1[0]
    g = h - (m1[0] + s1 * n2[0])
    y2 = solve(g)
    rr = dot(a0, m0) + 2.0 * dot(a1, m1) + s1 * dot(a1, n2)
    re = dot(a0, m1) + 2.0 * dot(a1, m2) + dot(a1, l3)
    ee = dot(a0, m2) + 2.0 * dot(a1, m3) + dot(a1, l4)
    s2 = (rr - re - over_m(y2 * h)) / (rr - 2.0 * re + ee - over_m(y2 * g))

    half = 0.5 * E3 * E3
    weights_r, weights_x = [], []
    for i in range(2):
        extra = s2 * y2 if i == 0 else 0.0
        weights_r.append((
            (1.0 - s2) * a0[i] + extra + half * s2 * a1[i],
            E3 * ((1.0 - s2) * a1[i] + s2 * a0[i]),
            half * s2 * a1[i],
        ))
        d0 = s1 * a[i] + s2 * a0[i]
        d1 = E3 * s2 * a1[i]
        weights_x.append((
            P0 * d0,
            P1 * d0 + (0.5 * P2) * d1,
            P2 * d0 + (0.5 * P1) * d1,
            P0 * d1,
            (0.5 * P1) * d1,
            (0.5 * P2) * d1,
        ))
    direct = coeffs - s1 * y1 - s2 * y2
    levels_r = (0, 3, 6)
    solid_r = [sum(w * TS[j] for w, j in zip(ws, levels_r)) for ws in weights_r]
    solid_x = [sum(w * TS[j] for j, w in enumerate(ws)) for ws in weights_x]

    odd = [(sub // step) % 2 == 1 for step in (1, 2, 4)]

    def each_over_m(values):
        for n, step in enumerate((1, 2, 4)):
            merged = []
            for u, v in zip(values[0::2], values[1::2]):
                stay, move = jnp.where(odd[n], v, u), jnp.where(odd[n], u, v)
                merged.append(stay + pltpu.roll(move, step, 0))
            values = merged
        return values[0]

    def tile(i, carry):
        p, t = i // 4, i % 4
        rows = pl.ds(t * 8, 8)
        ff = fo[p, rows, :]
        base_x = guess[p, rows, :]
        parts_x, parts_r = [], []
        for q in range(8):
            b = t * 8 + q
            r = rm[p, b]
            dry = jnp.where(jnp.broadcast_to(ff[q : q + 1, :], (8, 128)) > 0.0, 0.0, r)
            us = [tm[j, p, b] for j in range(7)]
            vx = direct * r + solid_x[0] * dry
            for j in range(6):
                vx = vx + weights_x[0][j] * us[j]
            vr = solid_r[0] * dry
            for w, j in zip(weights_r[0], levels_r):
                vr = vr + w * us[j]
            parts_x.append(vx)
            parts_r.append(vr)
        base_x = base_x + each_over_m(parts_x)
        base_r = each_over_m(parts_r)
        dry = rs[p, rows, :]
        vs = [tr[j, p, rows, :] for j in range(7)]
        base_x = base_x + solid_x[1] * dry
        base_r = base_r + solid_r[1] * dry
        for j in range(6):
            base_x = base_x + weights_x[1][j] * vs[j]
        for w, j in zip(weights_r[1], levels_r):
            base_r = base_r + w * vs[j]
        out_x[p, rows, :] = base_x
        out_r[p, rows, :] = base_r
        return carry

    lax.fori_loop(0, NA * 4, tile, 0)


def call(kernel, outs, scratch, limit, *args):
    return pl.pallas_call(
        kernel,
        out_shape=tuple(jax.ShapeDtypeStruct(s, f32) for s in outs),
        in_specs=[VMEM] * len(args),
        out_specs=tuple([VMEM] * len(outs)),
        scratch_shapes=[pltpu.VMEM(s, f32) for s in scratch],
        compiler_params=pltpu.CompilerParams(vmem_limit_bytes=limit),
    )(*args)


def local(right_side, first_guess, recycled, heights, ground_codes):
    mib = 1 << 20
    outs = ((NA * NB * K, 128), (4, 8, 128), (XTILES, 8, 128), (XTILES, 8, 128),
            (YTILES, 8, 128), (YTILES, 8, 128))
    rm, gnd, sxp, sxm, syp, sym = pl.pallas_call(
        pack_kernel,
        out_shape=tuple(jax.ShapeDtypeStruct(s, f32) for s in outs),
        in_specs=[pl.BlockSpec(memory_space=pl.ANY)] * 5,
        out_specs=tuple([VMEM] * len(outs)),
        scratch_shapes=[
            pltpu.VMEM((K, NA, NB, 128), jnp.bfloat16),
            pltpu.VMEM((NA, NB, 128), f32),
            pltpu.VMEM((NA, NB, 128), f32),
            pltpu.VMEM((NA, NB), jnp.int32),
            pltpu.VMEM((NA, NB), jnp.int32),
            pltpu.SemaphoreType.DMA((K + 4,)),
        ],
        compiler_params=pltpu.CompilerParams(vmem_limit_bytes=48 * mib),
    )(recycled, first_guess, right_side, heights, ground_codes)
    rm = rm.reshape(NA, NB, K, 128)

    def shift(value, axis, way):
        size = lax.axis_size(axis)
        pairs = [(i, i + way) for i in range(size) if 0 <= i + way < size]
        return lax.ppermute(value, axis, pairs)

    fxm, fxp = shift(sxp, "gx", 1), shift(sxm, "gx", -1)
    fym, fyp = shift(syp, "gy", 1), shift(sym, "gy", -1)
    cp, cm = call(
        corner_kernel, ((CTILES, 8, 128), (CTILES, 8, 128)), (), 16 * mib, fxm, fxp
    )
    cym, cyp = shift(cp, "gy", 1), shift(cm, "gy", -1)
    wide, flat = (PA, PB, 8, 128), (PA, QB, 128)
    pay, tm, tr, rs, fo = call(
        main_kernel,
        ((256, 2, 128), (7, NA, NB, 8, 128), (7, NA, NB, 128), (NA, NB, 128),
         (NA, NB, 128)),
        (wide, wide, wide, wide, flat, flat, flat, flat, (2, 128, 128), (2, 128, 128)),
        30 * mib,
        rm, first_guess, right_side, gnd, fxm, fxp, fym, fyp, cym, cyp,
    )
    got = lax.all_to_all(pay, ("gx", "gy"), 0, 0)
    return call(
        tail_kernel,
        ((NA, NB, 128), (NA, NB, 128)),
        (),
        8 * mib,
        got, rm, first_guess, tm, tr, rs, fo,
    )


def solution(mesh):
    placed = (
        P("gx", "gy", None),
        P("gx", "gy", None),
        P(None, "gx", "gy", None),
        P("gx", "gy"),
        P("gx", "gy"),
    )
    return jax.shard_map(
        local,
        mesh=mesh,
        in_specs=placed,
        out_specs=(P("gx", "gy", None), P("gx", "gy", None)),
        check_vma=False,
    )
```

```python
import jax
import jax.numpy as jnp
from jax import lax
from jax.experimental import pallas as pl
from jax.experimental.pallas import tpu as pltpu
from jax.sharding import PartitionSpec as P

NZ = 128
K = 8
H = 7
NA = 16
NB = 32
PA = NA + 2 * H
PB = NB + 2 * H
QB = NB + 16

CENTER = 7.25
HALF = 6.75
SIGMA = CENTER / HALF
T3 = 4.0 * SIGMA**3 - 3.0 * SIGMA
E3 = 1.0 / T3
TWO = 2.0 / HALF
DRY = -100.0
SOLID = (CENTER - 1.0) / HALF
TS = [1.0, SOLID]
for _ in range(5):
    TS.append(2.0 * SOLID * TS[-1] - TS[-2])
P0 = (4.0 * SIGMA**2 - 1.0) / (HALF * T3)
P1 = 4.0 * SIGMA / (HALF * T3)
P2 = 2.0 / (HALF * T3)

XR, XG, XS, XN = 0, 224, 252, 280
XTILES = 282
YR, YG, YS, YN = 0, 112, 128, 144
YTILES = 148
TRI = [(d, e) for d in range(1, H) for e in range(1, H + 1 - d)]
CG, CS, CN = len(TRI), len(TRI) + 7, len(TRI) + 14
CHALF = len(TRI) + 16
CTILES = 2 * CHALF

f32 = jnp.float32
VMEM = pl.BlockSpec(memory_space=pltpu.VMEM)


def vectors_kernel(rec, rm, sxp, sxm, syp, sym):
    for m in range(K):

        def body(a, carry, m=m):
            rm[pl.ds(a * (NB * K) + m, NB, stride=K), :] = rec[m, a].astype(f32)
            return carry

        lax.fori_loop(0, NA, body, 0)
    for out, lo in ((sxp, NA - H), (sxm, 0)):
        for i in range(H):
            for b in range(NB):
                at = ((lo + i) * NB + b) * K
                out[XR + i * NB + b] = rm[at : at + K, :]
    for out, lo in ((syp, NB - H), (sym, 0)):
        for a in range(NA):
            for i in range(H):
                at = (a * NB + lo + i) * K
                out[YR + a * H + i] = rm[at : at + K, :]


def rest_kernel(guess, right, heights, codes, _p, _m, _q, _n, gnd, sxp, sxm, syp, sym):
    for t in range(4):
        gnd[t] = jnp.zeros((8, 128), f32)
    for t in range(2):
        gnd[t, :, 0:NB] = (NZ - heights[8 * t : 8 * t + 8, :]).astype(f32)
        gnd[2 + t, :, 0:NB] = codes[8 * t : 8 * t + 8, :].astype(f32)
    for out, lo in ((sxp, NA - H), (sxm, 0)):
        for i in range(H):
            for t in range(4):
                out[XG + i * 4 + t] = guess[lo + i, 8 * t : 8 * t + 8, :]
                out[XS + i * 4 + t] = right[lo + i, 8 * t : 8 * t + 8, :]
        for t in range(2):
            out[XN + t] = jnp.zeros((8, 128), f32)
        out[XN, 0:H, 0:NB] = (NZ - heights[lo : lo + H, :]).astype(f32)
        out[XN + 1, 0:H, 0:NB] = codes[lo : lo + H, :].astype(f32)
    for out, tile in ((syp, 3), (sym, 0)):
        for a in range(NA):
            out[YG + a] = guess[a, 8 * tile : 8 * tile + 8, :]
            out[YS + a] = right[a, 8 * tile : 8 * tile + 8, :]
        for t in range(4):
            out[YN + t] = gnd[t]


def corner_row(side, d):
    return H - d if side == 0 else d - 1


def corner_kernel(fxm, fxp, cp, cm):
    for out, high in ((cp, True), (cm, False)):
        for side, src in ((0, fxm), (1, fxp)):
            base = side * CHALF
            for n, (d, e) in enumerate(TRI):
                b = NB - e if high else e - 1
                out[base + n] = src[XR + corner_row(side, d) * NB + b]
            tile = 3 if high else 0
            for i in range(H):
                out[base + CG + i] = src[XG + i * 4 + tile]
                out[base + CS + i] = src[XS + i * 4 + tile]
            out[base + CN] = src[XN]
            out[base + CN + 1] = src[XN + 1]


def widen(mid, left, right):
    lane = lax.broadcasted_iota(jnp.int32, (8, 128), 1)
    out = jnp.where((lane >= 8) & (lane < 40), pltpu.roll(mid, 8, 1), 0.0)
    if left is not None:
        out = jnp.where(lane < 8, pltpu.roll(left, 104, 1), out)
        moved = pltpu.roll(right, 40, 1)
        out = jnp.where((lane >= 40) & (lane < 48), moved, out)
    return out


def bounds():
    lane48 = lax.broadcasted_iota(jnp.int32, (QB, 128), 1)
    return lane48, lane48 > 0, lane48 < NZ - 1


def around(ref, a, c):
    _, low48, high48 = bounds()
    s = ref[a - 1] + ref[a + 1]
    s = s + pltpu.roll(c, 1, 0) + pltpu.roll(c, QB - 1, 0)
    s = s + jnp.where(low48, pltpu.roll(c, 1, 1), 0.0)
    return s + jnp.where(high48, pltpu.roll(c, NZ - 1, 1), 0.0)


def ground(gs, gt, fn, en, rows, gnd, fx=None, fy=None, cy=None):
    nothing = (None, None)
    for q in range(2):
        gs[q] = jnp.zeros((128, 128), f32)
        if fx is not None:
            sides = nothing if cy is None else [c[CN + q] for c in cy]
            gs[q, 0:8, :] = widen(fx[0][XN + q], *sides)
        for t in range(2):
            sides = nothing if fy is None else [f[YN + 2 * q + t] for f in fy]
            gs[q, H + 8 * t : H + 8 * t + 8, :] = widen(gnd[2 * q + t], *sides)
        if fx is not None:
            sides = nothing if cy is None else [c[CHALF + CN + q] for c in cy]
            gs[q, H + NA : H + NA + 8, :] = widen(fx[1][XN + q], *sides)
        gt[q, :, 0:32] = gs[q, 0:32, :].T
    lane48, low48, high48 = bounds()
    for a in rows:
        g = jnp.broadcast_to(gt[0, 0:QB, a : a + 1], (QB, 128))
        c = jnp.broadcast_to(gt[1, 0:QB, a : a + 1], (QB, 128))
        fn[a] = jnp.where(lane48.astype(f32) >= NZ - g, 1.0, 0.0)
        bottom = jnp.where(c == 1.0, 0.5, jnp.where(c == 2.0, 2.0, 0.0))
        en[a] = jnp.where(low48, 0.0, bottom) + jnp.where(high48, 0.0, 1.0)


def coefficients(fn, en, em, lo, hi, columns):
    def body(a, carry):
        fluid = fn[a]
        e = jnp.where(fluid > 0.0, (CENTER - around(fn, a, fluid) - en[a]) * TWO, DRY)
        en[a] = e
        for b in columns:
            em[a, b] = jnp.broadcast_to(e[b + 1 : b + 2, :], (8, 128))
        return carry

    lax.fori_loop(lo, hi, body, 0)


def flags(fn, em, a, columns):
    f = jnp.where(fn[a] > 0.0, 0.0, DRY)
    for b in columns:
        em[a, b] = jnp.broadcast_to(f[b + 1 : b + 2, :], (8, 128))


def keep(ua, em, a, b, value):
    ua[a, b] = jnp.where(em[a, b] > 0.5 * DRY, value, 0.0)


def sweep(level, src, dst, em, tm, lo_a, hi_a, spans, more, unroll):
    lane = lax.broadcasted_iota(jnp.int32, (8, 128), 1)
    low8, high8 = lane > 0, lane < NZ - 1

    def row(a, own):
        for lo_b, hi_b in spans:
            before, here = src[a, lo_b - 1], src[a, lo_b]
            for b in range(lo_b, hi_b):
                after = src[a, b + 1]
                s = (src[a - 1, b] + src[a + 1, b]) + (before + after)
                s = s + jnp.where(low8, pltpu.roll(here, 1, 1), 0.0)
                s = s + jnp.where(high8, pltpu.roll(here, NZ - 1, 1), 0.0)
                e = em[a, b]
                two = jnp.where(e > 0.5 * DRY, e * here + TWO * s, 0.0)
                if level == 0:
                    out = CENTER * here - (0.5 * HALF) * two
                elif level == 1:
                    out = 0.5 * two
                else:
                    out = two - dst[a, b]
                dst[a, b] = out
                if own and H <= b < H + NB:
                    tm[level, a - H, b - H] = out
                before, here = here, after
        if more is not None:
            more(a, own)

    for lo, hi, own in ((lo_a, H, False), (H, H + NA, True), (H + NA, hi_a, False)):
        lo, hi = max(lo, lo_a), min(hi, hi_a)
        count = max(hi - lo, 0) // unroll

        def body(i, carry, lo=lo, own=own):
            for n in range(unroll):
                row(lo + i * unroll + n, own)
            return carry

        if count:
            lax.fori_loop(0, count, body, 0)
        for a in range(lo + count * unroll, hi):
            row(a, own)


def levels(ua, ub, em, tm, region, more=None, unroll=2):
    for level in range(7):
        src, dst = (ua, ub) if level % 2 == 0 else (ub, ua)
        for lo_a, hi_a, spans in region(level):
            extra = None if more is None else more(level)
            sweep(level, src, dst, em, tm, lo_a, hi_a, spans, extra, unroll)


def inner_kernel(rm, gnd, ua, ub, em, tm, gs, gt, fn, en):
    first, last, left, right = H, H + NA - 1, H, H + NB - 1
    ground(gs, gt, fn, en, range(first, last + 1), gnd)
    coefficients(fn, en, em, first + 1, last, range(left + 1, right))
    for a in (first, last):
        flags(fn, em, a, range(left, right + 1))
    for a in range(first + 1, last):
        flags(fn, em, a, (left, right))

    def own(a, carry):
        for b in range(NB):
            keep(ua, em, H + a, H + b, rm[a, b])
        return carry

    lax.fori_loop(0, NA, own, 0)
    levels(ua, ub, em, tm, lambda j: [(8 + j, 22 - j, [(8 + j, 38 - j)])])


def strip_kernel(gnd, fxm, fxp, _a, _b, _e, _t, ua, ub, em, tm, gs, gt, fn, en):
    ground(gs, gt, fn, en, range(PA), gnd, (fxm, fxp))
    inside = range(H + 1, H + NB - 1)
    coefficients(fn, en, em, 1, H + 1, inside)
    coefficients(fn, en, em, H + NA - 1, PA - 1, inside)
    for a in (0, PA - 1):
        flags(fn, em, a, range(H, H + NB))
    for a in (*range(1, H), *range(H + NA, PA - 1)):
        flags(fn, em, a, (H, H + NB - 1))
    for top, src in ((0, fxm), (H + NA, fxp)):

        def rows(i, carry, src=src, top=top):
            for b in range(NB):
                keep(ua, em, top + i, H + b, src[XR + i * NB + b])
            return carry

        lax.fori_loop(0, H, rows, 0)

    def region(j):
        spans = [(8 + j, 38 - j)]
        return [(1 + j, 8 + j, spans), (22 - j, 29 - j, spans)]

    levels(ua, ub, em, tm, region)


def main_kernel(
    rm, guess, right, gnd, fxm, fxp, fym, fyp, cym, cyp, _a, _b, _e, _t,
    pay, tr, rs, fo, ua, ub, em, tm,
    fn, en, va, vb, gs, gt,
):
    lane = lax.broadcasted_iota(jnp.int32, (8, 128), 1)
    sub = lax.broadcasted_iota(jnp.int32, (8, 128), 0)
    ground(gs, gt, fn, en, range(PA), gnd, (fxm, fxp), (fym, fyp), (cym, cyp))
    rim = (*range(1, H + 1), *range(H + NB - 1, PB - 1))
    coefficients(fn, en, em, 1, PA - 1, rim)
    for a in (0, PA - 1):
        flags(fn, em, a, (*range(0, H), *range(H + NB, PB)))

    def ends(a, carry):
        flags(fn, em, a, (0, PB - 1))
        return carry

    lax.fori_loop(1, PA - 1, ends, 0)

    zero8 = jnp.zeros((8, 128), f32)
    for i in range(H):
        for b in range(H):
            for a in (i, H + NA + i):
                ua[a, b] = zero8
                ua[a, H + NB + b] = zero8
    for side in range(2):
        top = 0 if side == 0 else H + NA
        for n, (d, e) in enumerate(TRI):
            a = top + corner_row(side, d)
            keep(ua, em, a, H - e, cym[side * CHALF + n])
            keep(ua, em, a, H + NB + e - 1, cyp[side * CHALF + n])

    def sides(a, carry):
        for i in range(H):
            keep(ua, em, H + a, i, fym[YR + a * H + i])
            keep(ua, em, H + a, H + NB + i, fyp[YR + a * H + i])
        return carry

    lax.fori_loop(0, NA, sides, 0)

    for ref, mid, xo, yo, co in ((va, guess, XG, YG, CG), (vb, right, XS, YS, CS)):
        for a in range(NA):
            ref[H + a, 8:40, :] = mid[a]
            ref[H + a, 0:8, :] = fym[yo + a]
            ref[H + a, 40:48, :] = fyp[yo + a]
        for side, src in ((0, fxm), (1, fxp)):
            top = 0 if side == 0 else H + NA
            for i in range(H):
                for t in range(4):
                    ref[top + i, 8 + 8 * t : 16 + 8 * t, :] = src[xo + 4 * i + t]
                ref[top + i, 0:8, :] = cym[side * CHALF + co + i]
                ref[top + i, 40:48, :] = cyp[side * CHALF + co + i]
    for a in range(NA):
        f = fn[H + a, 8:40, :]
        fo[a] = f
        rs[a] = jnp.where(f > 0.0, 0.0, right[a] - guess[a])
    for a in range(PA):
        wet = fn[a] > 0.0
        va[a] = jnp.where(wet, va[a], 0.0)
        vb[a] = jnp.where(wet, vb[a], 0.0)

    def single(level):
        vsrc, vdst = (va, vb) if level % 2 == 0 else (vb, va)

        def row_of(a, own):
            c = vsrc[a]
            two = en[a] * c + fn[a] * TWO * around(vsrc, a, c)
            if level == 0:
                out = vdst[a] - (CENTER * c - (0.5 * HALF) * two)
            elif level == 1:
                out = 0.5 * two
            else:
                out = two - vdst[a]
            vdst[a] = out
            if own:
                tr[level, a - H] = out[8:40, :]

        return row_of

    def region(j):
        return [(1 + j, 29 - j, [(1 + j, 8 + j), (38 - j, 45 - j)])]

    levels(ua, ub, em, tm, region, single, 4)

    def row(tile, q):
        return jnp.broadcast_to(tile[q : q + 1, :], (8, 128))

    def joined(ref, at, dry):
        base = ref[(0, *at)]
        return (
            base + dry,
            ref[(3, *at)] + TS[3] * dry,
            (ref[(6, *at)] + base) + (TS[6] + 1.0) * dry,
        )

    def gather(i, carry):
        grams, cross, powers = carry
        a, t = i // 4, i % 4
        rows = pl.ds(t * 8, 8)
        r0, r3, r6 = joined(tr, (a, rows), rs[a, rows, :])
        pairs = (r0 * r0, r0 * r3, r0 * r6, r3 * r6, r6 * r6)
        powers = [p + v for p, v in zip(powers, pairs)]
        ff = fo[a, rows, :]
        for q in range(8):
            b = t * 8 + q
            dry = jnp.where(row(ff, q) > 0.0, 0.0, rm[a, b])
            t0, t3, t6 = joined(tm, (a, b), dry)
            new = [list(g) for g in grams]
            for k in range(5):
                v0 = t0 if k == 0 else pltpu.roll(t0, k, 0)
                v6 = t6 if k == 0 else pltpu.roll(t6, k, 0)
                for n, v in enumerate((t0 * v0, t3 * v0, t6 * v0, t3 * v6, t6 * v6)):
                    new[n][k] = new[n][k] + v
            grams = new
            w0, w3, w6 = row(r0, q), row(r3, q), row(r6, q)
            pairs = (t0 * w0, t0 * w3, t0 * w6, t3 * w6, t6 * w6)
            cross = [c + v for c, v in zip(cross, pairs)]
        return grams, cross, powers

    five = [zero8] * 5
    grams, cross, powers = lax.fori_loop(0, NA * 4, gather, ([five] * 5, five, five))
    scale = (1.0, E3, 0.5 * E3**2, 0.5 * E3**3, 0.25 * E3**4)
    packed = zero8
    for k in range(5):
        for r in range(5):
            value = scale[k] * jnp.sum(grams[k][r], axis=1, keepdims=True)
            packed = jnp.where(lane == 5 * k + r, value, packed)
        value = scale[k] * jnp.sum(cross[k], axis=1, keepdims=True)
        packed = jnp.where(lane == 25 + k, value, packed)
        value = scale[k] * jnp.sum(powers[k], axis=1, keepdims=True)
        value = jnp.sum(value, axis=0, keepdims=True)
        packed = jnp.where((lane == 30) & (sub == k), value, packed)
    packed = jnp.where(lane < 32, packed, 0.0)
    quarter = sub % 4
    moved = packed
    for i in range(1, 4):
        moved = jnp.where(quarter == i, pltpu.roll(packed, 32 * i, 1), moved)
    upper = jnp.sum(jnp.where(sub < 4, moved, 0.0), axis=0, keepdims=True)
    lower = jnp.sum(jnp.where(sub < 4, 0.0, moved), axis=0, keepdims=True)
    both = jnp.concatenate([upper, lower], axis=0)
    pay[...] = jnp.broadcast_to(both[None], pay.shape)


def tail_kernel(got, rm, guess, tm, tr, rs, fo, out_x, out_r):
    lane = lax.broadcasted_iota(jnp.int32, (8, 128), 1)
    sub = lax.broadcasted_iota(jnp.int32, (8, 128), 0)
    total = jnp.sum(got[...], axis=0)
    spread = jnp.where(
        sub < 4,
        jnp.broadcast_to(total[0:1, :], (8, 128)),
        jnp.broadcast_to(total[1:2, :], (8, 128)),
    )
    quarter = sub % 4
    packed = spread
    for i in range(1, 4):
        packed = jnp.where(quarter == i, pltpu.roll(spread, 128 - 32 * i, 1), packed)

    def column(j):
        return jnp.broadcast_to(packed[:, j : j + 1], (8, 128))

    def over_m(v):
        return jnp.broadcast_to(jnp.sum(v, axis=0, keepdims=True), (8, 128))

    diag = [[column(5 * k + r) for r in range(5)] for k in range(5)]
    cross = [column(25 + k) for k in range(5)]
    powers = column(30)
    rho = [over_m(jnp.where(sub == k, powers, 0.0)) for k in range(5)]

    def times(k, v):
        out = diag[k][0] * v
        for r in range(1, 5):
            out = out + diag[k][r] * pltpu.roll(v, r, 0)
        for r in range(1, 4):
            out = out + pltpu.roll(diag[k][r] * v, 8 - r, 0)
        return out

    mat = jnp.where(lane == sub + 8, 1.0, 0.0)
    for r in range(5):
        mat = jnp.where(lane == (sub + 8 - r) % 8, diag[0][r], mat)
    for r in range(1, 4):
        mat = jnp.where(lane == (sub + r) % 8, pltpu.roll(diag[0][r], 8 - r, 0), mat)
    for k in range(8):
        pivot_row = jnp.broadcast_to(mat[k : k + 1, :], (8, 128))
        pivot_row = pivot_row / jnp.broadcast_to(pivot_row[:, k : k + 1], (8, 128))
        factor = jnp.broadcast_to(mat[:, k : k + 1], (8, 128))
        mat = jnp.where(sub == k, pivot_row, mat - factor * pivot_row)
    inverse = jnp.where((lane >= 8) & (lane < 16), mat, 0.0)

    def solve(v):
        flat = over_m(jnp.where(lane == sub + 8, v, 0.0))
        return jnp.broadcast_to(
            jnp.sum(inverse * flat, axis=1, keepdims=True), (8, 128)
        )

    def apply(k, v):
        return times(k, v[0]) + cross[k] * v[1], over_m(cross[k] * v[0]) + rho[k] * v[1]

    def dot(u, v):
        return over_m(u[0] * v[0]) + u[1] * v[1]

    coeffs = solve(cross[0])
    one = jnp.ones((8, 128), f32)
    a = (-coeffs, one)
    n0, n1, n2 = apply(0, a), apply(1, a), apply(2, a)
    g = n0[0] - n1[0]
    y1 = solve(g)
    rr, re, ee = dot(a, n0), dot(a, n1), dot(a, n2)
    s1 = (rr - re - over_m(y1 * n0[0])) / (rr - 2.0 * re + ee - over_m(y1 * g))
    a0 = ((1.0 - s1) * a[0] + s1 * y1, (1.0 - s1) * a[1])
    a1 = (s1 * a[0], s1 * a[1])
    m0, m1, m2, m3 = apply(0, a0), apply(1, a0), apply(2, a0), apply(3, a0)
    l3, l4 = apply(3, a1), apply(4, a1)
    h = m0[0] + s1 * n1[0]
    g = h - (m1[0] + s1 * n2[0])
    y2 = solve(g)
    rr = dot(a0, m0) + 2.0 * dot(a1, m1) + s1 * dot(a1, n2)
    re = dot(a0, m1) + 2.0 * dot(a1, m2) + dot(a1, l3)
    ee = dot(a0, m2) + 2.0 * dot(a1, m3) + dot(a1, l4)
    s2 = (rr - re - over_m(y2 * h)) / (rr - 2.0 * re + ee - over_m(y2 * g))

    half = 0.5 * E3 * E3
    weights_r, weights_x = [], []
    for i in range(2):
        extra = s2 * y2 if i == 0 else 0.0
        weights_r.append((
            (1.0 - s2) * a0[i] + extra + half * s2 * a1[i],
            E3 * ((1.0 - s2) * a1[i] + s2 * a0[i]),
            half * s2 * a1[i],
        ))
        d0 = s1 * a[i] + s2 * a0[i]
        d1 = E3 * s2 * a1[i]
        weights_x.append((
            P0 * d0,
            P1 * d0 + (0.5 * P2) * d1,
            P2 * d0 + (0.5 * P1) * d1,
            P0 * d1,
            (0.5 * P1) * d1,
            (0.5 * P2) * d1,
        ))
    direct = coeffs - s1 * y1 - s2 * y2
    levels_r = (0, 3, 6)
    solid_r = [sum(w * TS[j] for w, j in zip(ws, levels_r)) for ws in weights_r]
    solid_x = [sum(w * TS[j] for j, w in enumerate(ws)) for ws in weights_x]

    odd = [(sub // step) % 2 == 1 for step in (1, 2, 4)]

    def each_over_m(values):
        for n, step in enumerate((1, 2, 4)):
            merged = []
            for u, v in zip(values[0::2], values[1::2]):
                stay, move = jnp.where(odd[n], v, u), jnp.where(odd[n], u, v)
                merged.append(stay + pltpu.roll(move, step, 0))
            values = merged
        return values[0]

    def tile(i, carry):
        p, t = i // 4, i % 4
        rows = pl.ds(t * 8, 8)
        ff = fo[p, rows, :]
        base_x = guess[p, rows, :]
        parts_x, parts_r = [], []
        for q in range(8):
            b = t * 8 + q
            r = rm[p, b]
            dry = jnp.where(jnp.broadcast_to(ff[q : q + 1, :], (8, 128)) > 0.0, 0.0, r)
            us = [tm[j, p, b] for j in range(7)]
            vx = direct * r + solid_x[0] * dry
            for j in range(6):
                vx = vx + weights_x[0][j] * us[j]
            vr = solid_r[0] * dry
            for w, j in zip(weights_r[0], levels_r):
                vr = vr + w * us[j]
            parts_x.append(vx)
            parts_r.append(vr)
        base_x = base_x + each_over_m(parts_x)
        base_r = each_over_m(parts_r)
        dry = rs[p, rows, :]
        vs = [tr[j, p, rows, :] for j in range(7)]
        base_x = base_x + solid_x[1] * dry
        base_r = base_r + solid_r[1] * dry
        for j in range(6):
            base_x = base_x + weights_x[1][j] * vs[j]
        for w, j in zip(weights_r[1], levels_r):
            base_r = base_r + w * vs[j]
        out_x[p, rows, :] = base_x
        out_r[p, rows, :] = base_r
        return carry

    lax.fori_loop(0, NA * 4, tile, 0)


def call(kernel, outs, scratch, limit, *args, aliases=None, cost=None):
    return pl.pallas_call(
        kernel,
        out_shape=tuple(jax.ShapeDtypeStruct(s, f32) for s in outs),
        in_specs=[VMEM] * len(args),
        out_specs=tuple([VMEM] * len(outs)),
        scratch_shapes=[pltpu.VMEM(s, f32) for s in scratch],
        input_output_aliases=aliases or {},
        cost_estimate=cost,
        compiler_params=pltpu.CompilerParams(vmem_limit_bytes=limit),
    )(*args)


def local(right_side, first_guess, recycled, heights, ground_codes):
    mib = 1 << 20
    faces = ((XTILES, 8, 128), (XTILES, 8, 128), (YTILES, 8, 128), (YTILES, 8, 128))
    rm, *sends = call(
        vectors_kernel, ((NA * NB * K, 128), *faces), (), 4 * mib, recycled
    )
    gnd, sxp, sxm, syp, sym = call(
        rest_kernel, ((4, 8, 128), *faces), (), 4 * mib,
        first_guess, right_side, heights, ground_codes, *sends,
        aliases={4: 1, 5: 2, 6: 3, 7: 4},
    )
    rm = rm.reshape(NA, NB, K, 128)

    def shift(value, axis, way):
        size = lax.axis_size(axis)
        pairs = [(i, i + way) for i in range(size) if 0 <= i + way < size]
        return lax.ppermute(value, axis, pairs)

    wide, flat = (PA, PB, 8, 128), (PA, QB, 128)
    fields = (wide, wide, wide, (7, NA, NB, 8, 128))
    small = ((2, 128, 128), (2, 128, 128), flat, flat)
    long = pl.CostEstimate(flops=10**10, bytes_accessed=4 * 10**7, transcendentals=0)
    fxm, fxp = shift(sxp, "gx", 1), shift(sxm, "gx", -1)
    fym, fyp = shift(syp, "gy", 1), shift(sym, "gy", -1)
    state = call(inner_kernel, fields, small, 8 * mib, rm, gnd, cost=long)
    cp, cm = call(
        corner_kernel, ((CTILES, 8, 128), (CTILES, 8, 128)), (), 8 * mib, fxm, fxp
    )
    cym, cyp = shift(cp, "gy", 1), shift(cm, "gy", -1)
    state = call(
        strip_kernel, fields, small, 8 * mib, gnd, fxm, fxp, *state,
        aliases={3: 0, 4: 1, 5: 2, 6: 3}, cost=long,
    )
    pay, tr, rs, fo, _, _, _, tm = call(
        main_kernel,
        ((256, 2, 128), (7, NA, NB, 128), (NA, NB, 128), (NA, NB, 128), *fields),
        (flat, flat, flat, flat, (2, 128, 128), (2, 128, 128)),
        8 * mib,
        rm, first_guess, right_side, gnd, fxm, fxp, fym, fyp, cym, cyp, *state,
        aliases={10: 4, 11: 5, 12: 6, 13: 7},
    )
    got = lax.all_to_all(pay, ("gx", "gy"), 0, 0)
    return call(
        tail_kernel,
        ((NA, NB, 128), (NA, NB, 128)),
        (),
        8 * mib,
        got, rm, first_guess, tm, tr, rs, fo,
    )


def solution(mesh):
    placed = (
        P("gx", "gy", None),
        P("gx", "gy", None),
        P(None, "gx", "gy", None),
        P("gx", "gy"),
        P("gx", "gy"),
    )
    return jax.shard_map(
        local,
        mesh=mesh,
        in_specs=placed,
        out_specs=(P("gx", "gy", None), P("gx", "gy", None)),
        check_vma=False,
    )
```

```python
import jax
import jax.numpy as jnp
from jax import lax
from jax.experimental import pallas as pl
from jax.experimental.pallas import tpu as pltpu
from jax.sharding import PartitionSpec as P

NZ = 128
K = 8
H = 7
NA = 16
NB = 32
PA = NA + 2 * H
PB = NB + 2 * H
QB = NB + 16

CENTER = 7.25
HALF = 6.75
SIGMA = CENTER / HALF
T3 = 4.0 * SIGMA**3 - 3.0 * SIGMA
E3 = 1.0 / T3
TWO = 2.0 / HALF
DRY = -100.0
SOLID = (CENTER - 1.0) / HALF
TS = [1.0, SOLID]
for _ in range(5):
    TS.append(2.0 * SOLID * TS[-1] - TS[-2])
P0 = (4.0 * SIGMA**2 - 1.0) / (HALF * T3)
P1 = 4.0 * SIGMA / (HALF * T3)
P2 = 2.0 / (HALF * T3)

XR, XG, XS, XN = 0, 224, 252, 280
XTILES = 282
YR, YG, YS, YN = 0, 112, 128, 144
YTILES = 148
TRI = [(d, e) for d in range(1, H) for e in range(1, H + 1 - d)]
CG, CS, CN = len(TRI), len(TRI) + 7, len(TRI) + 14
CHALF = len(TRI) + 16
CTILES = 2 * CHALF

f32 = jnp.float32
VMEM = pl.BlockSpec(memory_space=pltpu.VMEM)


def vectors_kernel(rec, rm, sxp, sxm, syp, sym):
    for m in range(K):

        def body(a, carry, m=m):
            rm[pl.ds(a * (NB * K) + m, NB, stride=K), :] = rec[m, a].astype(f32)
            return carry

        lax.fori_loop(0, NA, body, 0)
    for out, lo in ((sxp, NA - H), (sxm, 0)):
        for i in range(H):
            for b in range(NB):
                at = ((lo + i) * NB + b) * K
                out[XR + i * NB + b] = rm[at : at + K, :]
    for out, lo in ((syp, NB - H), (sym, 0)):
        for a in range(NA):
            for i in range(H):
                at = (a * NB + lo + i) * K
                out[YR + a * H + i] = rm[at : at + K, :]


def rest_kernel(pair, columns, _p, _m, _q, _n, gnd, sxp, sxm, syp, sym):
    guess, right, heights, codes = pair.at[0], pair.at[1], columns.at[0], columns.at[1]
    for t in range(4):
        gnd[t] = jnp.zeros((8, 128), f32)
    for t in range(2):
        gnd[t, :, 0:NB] = (NZ - heights[8 * t : 8 * t + 8, :]).astype(f32)
        gnd[2 + t, :, 0:NB] = codes[8 * t : 8 * t + 8, :].astype(f32)
    for out, lo in ((sxp, NA - H), (sxm, 0)):
        for i in range(H):
            for t in range(4):
                out[XG + i * 4 + t] = guess[lo + i, 8 * t : 8 * t + 8, :]
                out[XS + i * 4 + t] = right[lo + i, 8 * t : 8 * t + 8, :]
        for t in range(2):
            out[XN + t] = jnp.zeros((8, 128), f32)
        out[XN, 0:H, 0:NB] = (NZ - heights[lo : lo + H, :]).astype(f32)
        out[XN + 1, 0:H, 0:NB] = codes[lo : lo + H, :].astype(f32)
    for out, tile in ((syp, 3), (sym, 0)):
        for a in range(NA):
            out[YG + a] = guess[a, 8 * tile : 8 * tile + 8, :]
            out[YS + a] = right[a, 8 * tile : 8 * tile + 8, :]
        for t in range(4):
            out[YN + t] = gnd[t]


def corner_row(side, d):
    return H - d if side == 0 else d - 1


def corner_kernel(fxm, fxp, cp, cm):
    for out, high in ((cp, True), (cm, False)):
        for side, src in ((0, fxm), (1, fxp)):
            base = side * CHALF
            for n, (d, e) in enumerate(TRI):
                b = NB - e if high else e - 1
                out[base + n] = src[XR + corner_row(side, d) * NB + b]
            tile = 3 if high else 0
            for i in range(H):
                out[base + CG + i] = src[XG + i * 4 + tile]
                out[base + CS + i] = src[XS + i * 4 + tile]
            out[base + CN] = src[XN]
            out[base + CN + 1] = src[XN + 1]


def widen(mid, left, right):
    lane = lax.broadcasted_iota(jnp.int32, (8, 128), 1)
    out = jnp.where((lane >= 8) & (lane < 40), pltpu.roll(mid, 8, 1), 0.0)
    if left is not None:
        out = jnp.where(lane < 8, pltpu.roll(left, 104, 1), out)
        moved = pltpu.roll(right, 40, 1)
        out = jnp.where((lane >= 40) & (lane < 48), moved, out)
    return out


def bounds():
    lane48 = lax.broadcasted_iota(jnp.int32, (QB, 128), 1)
    return lane48, lane48 > 0, lane48 < NZ - 1


def around(ref, a, c):
    _, low48, high48 = bounds()
    s = ref[a - 1] + ref[a + 1]
    s = s + pltpu.roll(c, 1, 0) + pltpu.roll(c, QB - 1, 0)
    s = s + jnp.where(low48, pltpu.roll(c, 1, 1), 0.0)
    return s + jnp.where(high48, pltpu.roll(c, NZ - 1, 1), 0.0)


def ground(gs, gt, fn, en, rows, gnd, fx=None, fy=None, cy=None):
    nothing = (None, None)
    for q in range(2):
        gs[q] = jnp.zeros((128, 128), f32)
        if fx is not None:
            sides = nothing if cy is None else [c[CN + q] for c in cy]
            gs[q, 0:8, :] = widen(fx[0][XN + q], *sides)
        for t in range(2):
            sides = nothing if fy is None else [f[YN + 2 * q + t] for f in fy]
            gs[q, H + 8 * t : H + 8 * t + 8, :] = widen(gnd[2 * q + t], *sides)
        if fx is not None:
            sides = nothing if cy is None else [c[CHALF + CN + q] for c in cy]
            gs[q, H + NA : H + NA + 8, :] = widen(fx[1][XN + q], *sides)
        gt[q, :, 0:32] = gs[q, 0:32, :].T
    lane48, low48, high48 = bounds()
    for a in rows:
        g = jnp.broadcast_to(gt[0, 0:QB, a : a + 1], (QB, 128))
        c = jnp.broadcast_to(gt[1, 0:QB, a : a + 1], (QB, 128))
        fn[a] = jnp.where(lane48.astype(f32) >= NZ - g, 1.0, 0.0)
        bottom = jnp.where(c == 1.0, 0.5, jnp.where(c == 2.0, 2.0, 0.0))
        en[a] = jnp.where(low48, 0.0, bottom) + jnp.where(high48, 0.0, 1.0)


def coefficients(fn, en, em, lo, hi, columns):
    def body(a, carry):
        fluid = fn[a]
        e = jnp.where(fluid > 0.0, (CENTER - around(fn, a, fluid) - en[a]) * TWO, DRY)
        en[a] = e
        for b in columns:
            em[a, b] = jnp.broadcast_to(e[b + 1 : b + 2, :], (8, 128))
        return carry

    lax.fori_loop(lo, hi, body, 0)


def flags(fn, em, a, columns):
    f = jnp.where(fn[a] > 0.0, 0.0, DRY)
    for b in columns:
        em[a, b] = jnp.broadcast_to(f[b + 1 : b + 2, :], (8, 128))


def keep(ua, em, a, b, value):
    ua[a, b] = jnp.where(em[a, b] > 0.5 * DRY, value, 0.0)


def sweep(level, src, dst, em, tm, lo_a, hi_a, spans, more, unroll):
    lane = lax.broadcasted_iota(jnp.int32, (8, 128), 1)
    low8, high8 = lane > 0, lane < NZ - 1

    def row(a, own):
        for lo_b, hi_b in spans:
            before, here = src[a, lo_b - 1], src[a, lo_b]
            for b in range(lo_b, hi_b):
                after = src[a, b + 1]
                s = (src[a - 1, b] + src[a + 1, b]) + (before + after)
                s = s + jnp.where(low8, pltpu.roll(here, 1, 1), 0.0)
                s = s + jnp.where(high8, pltpu.roll(here, NZ - 1, 1), 0.0)
                e = em[a, b]
                two = jnp.where(e > 0.5 * DRY, e * here + TWO * s, 0.0)
                if level == 0:
                    out = CENTER * here - (0.5 * HALF) * two
                elif level == 1:
                    out = 0.5 * two
                else:
                    out = two - dst[a, b]
                dst[a, b] = out
                if own and H <= b < H + NB:
                    tm[level, a - H, b - H] = out
                before, here = here, after
        if more is not None:
            more(a, own)

    for lo, hi, own in ((lo_a, H, False), (H, H + NA, True), (H + NA, hi_a, False)):
        lo, hi = max(lo, lo_a), min(hi, hi_a)
        count = max(hi - lo, 0) // unroll

        def body(i, carry, lo=lo, own=own):
            for n in range(unroll):
                row(lo + i * unroll + n, own)
            return carry

        if count:
            lax.fori_loop(0, count, body, 0)
        for a in range(lo + count * unroll, hi):
            row(a, own)


def levels(ua, ub, em, tm, region, more=None, unroll=4):
    for level in range(7):
        src, dst = (ua, ub) if level % 2 == 0 else (ub, ua)
        for lo_a, hi_a, spans in region(level):
            extra = None if more is None else more(level)
            sweep(level, src, dst, em, tm, lo_a, hi_a, spans, extra, unroll)


def inner_kernel(rm, gnd, ua, ub, em, tm, gs, gt, fn, en):
    first, last, left, right = H, H + NA - 1, H, H + NB - 1
    ground(gs, gt, fn, en, range(first, last + 1), gnd)
    coefficients(fn, en, em, first + 1, last, range(left + 1, right))
    for a in (first, last):
        flags(fn, em, a, range(left, right + 1))
    for a in range(first + 1, last):
        flags(fn, em, a, (left, right))

    def own(a, carry):
        for b in range(NB):
            keep(ua, em, H + a, H + b, rm[a, b])
        return carry

    lax.fori_loop(0, NA, own, 0)
    levels(ua, ub, em, tm, lambda j: [(8 + j, 22 - j, [(8 + j, 38 - j)])])


def strip_kernel(gnd, fxm, fxp, _a, _b, _e, _t, ua, ub, em, tm, gs, gt, fn, en):
    ground(gs, gt, fn, en, range(PA), gnd, (fxm, fxp))
    inside = range(H + 1, H + NB - 1)
    coefficients(fn, en, em, 1, H + 1, inside)
    coefficients(fn, en, em, H + NA - 1, PA - 1, inside)
    for a in (0, PA - 1):
        flags(fn, em, a, range(H, H + NB))
    for a in (*range(1, H), *range(H + NA, PA - 1)):
        flags(fn, em, a, (H, H + NB - 1))
    for top, src in ((0, fxm), (H + NA, fxp)):

        def rows(i, carry, src=src, top=top):
            for b in range(NB):
                keep(ua, em, top + i, H + b, src[XR + i * NB + b])
            return carry

        lax.fori_loop(0, H, rows, 0)

    def region(j):
        spans = [(8 + j, 38 - j)]
        return [(1 + j, 8 + j, spans), (22 - j, 29 - j, spans)]

    levels(ua, ub, em, tm, region)


def main_kernel(
    rm, pair, gnd, fxm, fxp, fym, fyp, cym, cyp, _a, _b, _e, _t,
    pay, tr, rs, fo, ua, ub, em, tm,
    fn, en, va, vb, gs, gt, flat,
):
    lane = lax.broadcasted_iota(jnp.int32, (8, 128), 1)
    sub = lax.broadcasted_iota(jnp.int32, (8, 128), 0)
    guess, right = pair.at[0], pair.at[1]
    ground(gs, gt, fn, en, range(PA), gnd, (fxm, fxp), (fym, fyp), (cym, cyp))
    rim = (*range(1, H + 1), *range(H + NB - 1, PB - 1))
    coefficients(fn, en, em, 1, PA - 1, rim)
    for a in (0, PA - 1):
        flags(fn, em, a, (*range(0, H), *range(H + NB, PB)))

    def ends(a, carry):
        flags(fn, em, a, (0, PB - 1))
        return carry

    lax.fori_loop(1, PA - 1, ends, 0)

    zero8 = jnp.zeros((8, 128), f32)
    for i in range(H):
        for b in range(H):
            for a in (i, H + NA + i):
                ua[a, b] = zero8
                ua[a, H + NB + b] = zero8
    for side in range(2):
        top = 0 if side == 0 else H + NA
        for n, (d, e) in enumerate(TRI):
            a = top + corner_row(side, d)
            keep(ua, em, a, H - e, cym[side * CHALF + n])
            keep(ua, em, a, H + NB + e - 1, cyp[side * CHALF + n])

    def sides(a, carry):
        for i in range(H):
            keep(ua, em, H + a, i, fym[YR + a * H + i])
            keep(ua, em, H + a, H + NB + i, fyp[YR + a * H + i])
        return carry

    lax.fori_loop(0, NA, sides, 0)

    for ref, mid, xo, yo, co in ((va, guess, XG, YG, CG), (vb, right, XS, YS, CS)):
        for a in range(NA):
            ref[H + a, 8:40, :] = mid[a]
            ref[H + a, 0:8, :] = fym[yo + a]
            ref[H + a, 40:48, :] = fyp[yo + a]
        for side, src in ((0, fxm), (1, fxp)):
            top = 0 if side == 0 else H + NA
            for i in range(H):
                for t in range(4):
                    ref[top + i, 8 + 8 * t : 16 + 8 * t, :] = src[xo + 4 * i + t]
                ref[top + i, 0:8, :] = cym[side * CHALF + co + i]
                ref[top + i, 40:48, :] = cyp[side * CHALF + co + i]
    for a in range(NA):
        f = fn[H + a, 8:40, :]
        fo[a] = f
        rs[a] = jnp.where(f > 0.0, 0.0, right[a] - guess[a])
    for a in range(PA):
        wet = fn[a] > 0.0
        va[a] = jnp.where(wet, va[a], 0.0)
        vb[a] = jnp.where(wet, vb[a], 0.0)

    def single(level):
        vsrc, vdst = (va, vb) if level % 2 == 0 else (vb, va)

        def row_of(a, own):
            c = vsrc[a]
            two = en[a] * c + fn[a] * TWO * around(vsrc, a, c)
            if level == 0:
                out = vdst[a] - (CENTER * c - (0.5 * HALF) * two)
            elif level == 1:
                out = 0.5 * two
            else:
                out = two - vdst[a]
            vdst[a] = out
            if own:
                tr[level, a - H] = out[8:40, :]

        return row_of

    def region(j):
        return [(1 + j, 29 - j, [(1 + j, 8 + j), (38 - j, 45 - j)])]

    levels(ua, ub, em, tm, region, single)

    def joined(ref, at, dry):
        base = ref[(0, *at)]
        return (
            base + dry,
            ref[(3, *at)] + TS[3] * dry,
            (ref[(6, *at)] + base) + (TS[6] + 1.0) * dry,
        )

    def gather(i, carry):
        grams, cross, powers = carry
        a, t = i // 4, i % 4
        rows = pl.ds(t * 8, 8)
        r0, r3, r6 = joined(tr, (a, rows), rs[a, rows, :])
        pairs = (r0 * r0, r0 * r3, r0 * r6, r3 * r6, r6 * r6)
        powers = [p + v for p, v in zip(powers, pairs)]
        for n, value in enumerate((r0, r3, r6)):
            flat[n] = value
        for q in range(8):
            b = t * 8 + q
            dry = jnp.where(em[H + a, H + b] > 0.5 * DRY, 0.0, rm[a, b])
            t0, t3, t6 = joined(tm, (a, b), dry)
            new = [list(g) for g in grams]
            for k in range(5):
                v0 = t0 if k == 0 else pltpu.roll(t0, k, 0)
                v6 = t6 if k == 0 else pltpu.roll(t6, k, 0)
                for n, v in enumerate((t0 * v0, t3 * v0, t6 * v0, t3 * v6, t6 * v6)):
                    new[n][k] = new[n][k] + v
            grams = new
            w0, w3, w6 = [flat[n, pl.ds(q, 8, stride=0), :] for n in range(3)]
            pairs = (t0 * w0, t0 * w3, t0 * w6, t3 * w6, t6 * w6)
            cross = [c + v for c, v in zip(cross, pairs)]
        return grams, cross, powers

    five = [zero8] * 5
    grams, cross, powers = lax.fori_loop(0, NA * 4, gather, ([five] * 5, five, five))
    scale = (1.0, E3, 0.5 * E3**2, 0.5 * E3**3, 0.25 * E3**4)
    packed = zero8
    for k in range(5):
        for r in range(5):
            value = scale[k] * jnp.sum(grams[k][r], axis=1, keepdims=True)
            packed = jnp.where(lane == 5 * k + r, value, packed)
        value = scale[k] * jnp.sum(cross[k], axis=1, keepdims=True)
        packed = jnp.where(lane == 25 + k, value, packed)
        value = scale[k] * jnp.sum(powers[k], axis=1, keepdims=True)
        value = jnp.sum(value, axis=0, keepdims=True)
        packed = jnp.where((lane == 30) & (sub == k), value, packed)
    packed = jnp.where(lane < 32, packed, 0.0)
    quarter = sub % 4
    moved = packed
    for i in range(1, 4):
        moved = jnp.where(quarter == i, pltpu.roll(packed, 32 * i, 1), moved)
    upper = jnp.sum(jnp.where(sub < 4, moved, 0.0), axis=0, keepdims=True)
    lower = jnp.sum(jnp.where(sub < 4, 0.0, moved), axis=0, keepdims=True)
    both = jnp.concatenate([upper, lower], axis=0)
    pay[...] = jnp.broadcast_to(both[None], pay.shape)


def tail_kernel(got, rm, pair, tm, tr, rs, fo, out_x, out_r):
    lane = lax.broadcasted_iota(jnp.int32, (8, 128), 1)
    sub = lax.broadcasted_iota(jnp.int32, (8, 128), 0)
    total = jnp.sum(got[...], axis=0)
    spread = jnp.where(
        sub < 4,
        jnp.broadcast_to(total[0:1, :], (8, 128)),
        jnp.broadcast_to(total[1:2, :], (8, 128)),
    )
    quarter = sub % 4
    packed = spread
    for i in range(1, 4):
        packed = jnp.where(quarter == i, pltpu.roll(spread, 128 - 32 * i, 1), packed)

    def column(j):
        return jnp.broadcast_to(packed[:, j : j + 1], (8, 128))

    def over_m(v):
        return jnp.broadcast_to(jnp.sum(v, axis=0, keepdims=True), (8, 128))

    diag = [[column(5 * k + r) for r in range(5)] for k in range(5)]
    cross = [column(25 + k) for k in range(5)]
    powers = column(30)
    rho = [over_m(jnp.where(sub == k, powers, 0.0)) for k in range(5)]

    def times(k, v):
        out = diag[k][0] * v
        for r in range(1, 5):
            out = out + diag[k][r] * pltpu.roll(v, r, 0)
        for r in range(1, 4):
            out = out + pltpu.roll(diag[k][r] * v, 8 - r, 0)
        return out

    mat = jnp.where(lane == sub + 8, 1.0, 0.0)
    for r in range(5):
        mat = jnp.where(lane == (sub + 8 - r) % 8, diag[0][r], mat)
    for r in range(1, 4):
        mat = jnp.where(lane == (sub + r) % 8, pltpu.roll(diag[0][r], 8 - r, 0), mat)
    for k in range(8):
        pivot_row = jnp.broadcast_to(mat[k : k + 1, :], (8, 128))
        pivot_row = pivot_row / jnp.broadcast_to(pivot_row[:, k : k + 1], (8, 128))
        factor = jnp.broadcast_to(mat[:, k : k + 1], (8, 128))
        mat = jnp.where(sub == k, pivot_row, mat - factor * pivot_row)
    inverse = jnp.where((lane >= 8) & (lane < 16), mat, 0.0)

    def solve(v):
        flat = over_m(jnp.where(lane == sub + 8, v, 0.0))
        return jnp.broadcast_to(
            jnp.sum(inverse * flat, axis=1, keepdims=True), (8, 128)
        )

    def apply(k, v):
        return times(k, v[0]) + cross[k] * v[1], over_m(cross[k] * v[0]) + rho[k] * v[1]

    def dot(u, v):
        return over_m(u[0] * v[0]) + u[1] * v[1]

    coeffs = solve(cross[0])
    one = jnp.ones((8, 128), f32)
    a = (-coeffs, one)
    n0, n1, n2 = apply(0, a), apply(1, a), apply(2, a)
    g = n0[0] - n1[0]
    y1 = solve(g)
    rr, re, ee = dot(a, n0), dot(a, n1), dot(a, n2)
    s1 = (rr - re - over_m(y1 * n0[0])) / (rr - 2.0 * re + ee - over_m(y1 * g))
    a0 = ((1.0 - s1) * a[0] + s1 * y1, (1.0 - s1) * a[1])
    a1 = (s1 * a[0], s1 * a[1])
    m0, m1, m2, m3 = apply(0, a0), apply(1, a0), apply(2, a0), apply(3, a0)
    l3, l4 = apply(3, a1), apply(4, a1)
    h = m0[0] + s1 * n1[0]
    g = h - (m1[0] + s1 * n2[0])
    y2 = solve(g)
    rr = dot(a0, m0) + 2.0 * dot(a1, m1) + s1 * dot(a1, n2)
    re = dot(a0, m1) + 2.0 * dot(a1, m2) + dot(a1, l3)
    ee = dot(a0, m2) + 2.0 * dot(a1, m3) + dot(a1, l4)
    s2 = (rr - re - over_m(y2 * h)) / (rr - 2.0 * re + ee - over_m(y2 * g))

    half = 0.5 * E3 * E3
    weights_r, weights_x = [], []
    for i in range(2):
        extra = s2 * y2 if i == 0 else 0.0
        weights_r.append((
            (1.0 - s2) * a0[i] + extra + half * s2 * a1[i],
            E3 * ((1.0 - s2) * a1[i] + s2 * a0[i]),
            half * s2 * a1[i],
        ))
        d0 = s1 * a[i] + s2 * a0[i]
        d1 = E3 * s2 * a1[i]
        weights_x.append((
            P0 * d0,
            P1 * d0 + (0.5 * P2) * d1,
            P2 * d0 + (0.5 * P1) * d1,
            P0 * d1,
            (0.5 * P1) * d1,
            (0.5 * P2) * d1,
        ))
    direct = coeffs - s1 * y1 - s2 * y2
    levels_r = (0, 3, 6)
    solid_r = [sum(w * TS[j] for w, j in zip(ws, levels_r)) for ws in weights_r]
    solid_x = [sum(w * TS[j] for j, w in enumerate(ws)) for ws in weights_x]

    odd = [(sub // step) % 2 == 1 for step in (1, 2, 4)]

    def each_over_m(values):
        for n, step in enumerate((1, 2, 4)):
            merged = []
            for u, v in zip(values[0::2], values[1::2]):
                stay, move = jnp.where(odd[n], v, u), jnp.where(odd[n], u, v)
                merged.append(stay + pltpu.roll(move, step, 0))
            values = merged
        return values[0]

    def tile(i, carry):
        p, t = i // 4, i % 4
        rows = pl.ds(t * 8, 8)
        ff = fo[p, rows, :]
        base_x = pair[0, p, rows, :]
        parts_x, parts_r = [], []
        for q in range(8):
            b = t * 8 + q
            r = rm[p, b]
            dry = jnp.where(jnp.broadcast_to(ff[q : q + 1, :], (8, 128)) > 0.0, 0.0, r)
            us = [tm[j, p, b] for j in range(7)]
            vx = direct * r + solid_x[0] * dry
            for j in range(6):
                vx = vx + weights_x[0][j] * us[j]
            vr = solid_r[0] * dry
            for w, j in zip(weights_r[0], levels_r):
                vr = vr + w * us[j]
            parts_x.append(vx)
            parts_r.append(vr)
        base_x = base_x + each_over_m(parts_x)
        base_r = each_over_m(parts_r)
        dry = rs[p, rows, :]
        vs = [tr[j, p, rows, :] for j in range(7)]
        base_x = base_x + solid_x[1] * dry
        base_r = base_r + solid_r[1] * dry
        for j in range(6):
            base_x = base_x + weights_x[1][j] * vs[j]
        for w, j in zip(weights_r[1], levels_r):
            base_r = base_r + w * vs[j]
        out_x[p, rows, :] = base_x
        out_r[p, rows, :] = base_r
        return carry

    lax.fori_loop(0, NA * 4, tile, 0)


def call(kernel, outs, scratch, limit, *args, aliases=None, cost=None):
    return pl.pallas_call(
        kernel,
        out_shape=tuple(jax.ShapeDtypeStruct(s, f32) for s in outs),
        in_specs=[VMEM] * len(args),
        out_specs=tuple([VMEM] * len(outs)),
        scratch_shapes=[pltpu.VMEM(s, f32) for s in scratch],
        input_output_aliases=aliases or {},
        cost_estimate=cost,
        compiler_params=pltpu.CompilerParams(vmem_limit_bytes=limit),
    )(*args)


def local(right_side, first_guess, recycled, heights, ground_codes):
    mib = 1 << 20
    faces = ((XTILES, 8, 128), (XTILES, 8, 128), (YTILES, 8, 128), (YTILES, 8, 128))
    pair = jnp.stack([first_guess, right_side])
    columns = jnp.stack([heights, ground_codes])
    rm, *sends = call(
        vectors_kernel, ((NA * NB * K, 128), *faces), (), 4 * mib, recycled
    )
    gnd, sxp, sxm, syp, sym = call(
        rest_kernel, ((4, 8, 128), *faces), (), 4 * mib,
        pair, columns, *sends,
        aliases={2: 1, 3: 2, 4: 3, 5: 4},
    )
    rm = rm.reshape(NA, NB, K, 128)

    def shift(value, axis, way):
        size = lax.axis_size(axis)
        pairs = [(i, i + way) for i in range(size) if 0 <= i + way < size]
        return lax.ppermute(value, axis, pairs)

    wide, flat = (PA, PB, 8, 128), (PA, QB, 128)
    fields = (wide, wide, wide, (7, NA, NB, 8, 128))
    small = ((2, 128, 128), (2, 128, 128), flat, flat)
    long = pl.CostEstimate(flops=10**10, bytes_accessed=4 * 10**7, transcendentals=0)
    fxm, fxp = shift(sxp, "gx", 1), shift(sxm, "gx", -1)
    fym, fyp = shift(syp, "gy", 1), shift(sym, "gy", -1)
    state = call(inner_kernel, fields, small, 8 * mib, rm, gnd, cost=long)
    cp, cm = call(
        corner_kernel, ((CTILES, 8, 128), (CTILES, 8, 128)), (), 8 * mib, fxm, fxp
    )
    cym, cyp = shift(cp, "gy", 1), shift(cm, "gy", -1)
    state = call(
        strip_kernel, fields, small, 8 * mib, gnd, fxm, fxp, *state,
        aliases={3: 0, 4: 1, 5: 2, 6: 3}, cost=long,
    )
    pay, tr, rs, fo, _, _, _, tm = call(
        main_kernel,
        ((256, 2, 128), (7, NA, NB, 128), (NA, NB, 128), (NA, NB, 128), *fields),
        (flat, flat, flat, flat, (2, 128, 128), (2, 128, 128), (3, 8, 128)),
        8 * mib,
        rm, pair, gnd, fxm, fxp, fym, fyp, cym, cyp, *state,
        aliases={9: 4, 10: 5, 11: 6, 12: 7},
    )
    got = lax.all_to_all(pay, ("gx", "gy"), 0, 0)
    return call(
        tail_kernel,
        ((NA, NB, 128), (NA, NB, 128)),
        (),
        8 * mib,
        got, rm, pair, tm, tr, rs, fo,
    )


def solution(mesh):
    placed = (
        P("gx", "gy", None),
        P("gx", "gy", None),
        P(None, "gx", "gy", None),
        P("gx", "gy"),
        P("gx", "gy"),
    )
    return jax.shard_map(
        local,
        mesh=mesh,
        in_specs=placed,
        out_specs=(P("gx", "gy", None), P("gx", "gy", None)),
        check_vma=False,
    )
```

```python
import jax
import jax.numpy as jnp
from jax import lax
from jax.experimental import pallas as pl
from jax.experimental.pallas import tpu as pltpu
from jax.sharding import PartitionSpec as P

NZ = 128
K = 8
H = 7
NA = 16
NB = 32
PA = NA + 2 * H
PB = NB + 2 * H
QB = NB + 16

CENTER = 7.25
HALF = 6.75
SIGMA = CENTER / HALF
T3 = 4.0 * SIGMA**3 - 3.0 * SIGMA
E3 = 1.0 / T3
TWO = 2.0 / HALF
DRY = -100.0
SOLID = (CENTER - 1.0) / HALF
TS = [1.0, SOLID]
for _ in range(5):
    TS.append(2.0 * SOLID * TS[-1] - TS[-2])
P0 = (4.0 * SIGMA**2 - 1.0) / (HALF * T3)
P1 = 4.0 * SIGMA / (HALF * T3)
P2 = 2.0 / (HALF * T3)

XR, XG, XS, XN = 0, 224, 252, 280
XTILES = 282
YR, YG, YS, YN = 0, 112, 128, 144
YTILES = 148
TRI = [(d, e) for d in range(1, H) for e in range(1, H + 1 - d)]
CG, CS, CN = len(TRI), len(TRI) + 7, len(TRI) + 14
CHALF = len(TRI) + 16
CTILES = 2 * CHALF

f32 = jnp.float32
VMEM = pl.BlockSpec(memory_space=pltpu.VMEM)


def vectors_kernel(rec, rm, sxp, sxm, syp, sym):
    for m in range(K):

        def body(a, carry, m=m):
            rm[pl.ds(a * (NB * K) + m, NB, stride=K), :] = rec[m, a].astype(f32)
            return carry

        lax.fori_loop(0, NA, body, 0)
    for out, lo in ((sxp, NA - H), (sxm, 0)):
        for i in range(H):
            for b in range(NB):
                at = ((lo + i) * NB + b) * K
                out[XR + i * NB + b] = rm[at : at + K, :]
    for out, lo in ((syp, NB - H), (sym, 0)):
        for a in range(NA):
            for i in range(H):
                at = (a * NB + lo + i) * K
                out[YR + a * H + i] = rm[at : at + K, :]


def rest_kernel(guess, right, heights, codes, _p, _m, _q, _n, gnd, sxp, sxm, syp, sym):
    for t in range(4):
        gnd[t] = jnp.zeros((8, 128), f32)
    for t in range(2):
        gnd[t, :, 0:NB] = (NZ - heights[8 * t : 8 * t + 8, :]).astype(f32)
        gnd[2 + t, :, 0:NB] = codes[8 * t : 8 * t + 8, :].astype(f32)
    for out, lo in ((sxp, NA - H), (sxm, 0)):
        for i in range(H):
            for t in range(4):
                out[XG + i * 4 + t] = guess[lo + i, 8 * t : 8 * t + 8, :]
                out[XS + i * 4 + t] = right[lo + i, 8 * t : 8 * t + 8, :]
        for t in range(2):
            out[XN + t] = jnp.zeros((8, 128), f32)
        out[XN, 0:H, 0:NB] = (NZ - heights[lo : lo + H, :]).astype(f32)
        out[XN + 1, 0:H, 0:NB] = codes[lo : lo + H, :].astype(f32)
    for out, tile in ((syp, 3), (sym, 0)):
        for a in range(NA):
            out[YG + a] = guess[a, 8 * tile : 8 * tile + 8, :]
            out[YS + a] = right[a, 8 * tile : 8 * tile + 8, :]
        for t in range(4):
            out[YN + t] = gnd[t]


def corner_row(side, d):
    return H - d if side == 0 else d - 1


def corner_kernel(fxm, fxp, cp, cm):
    for out, high in ((cp, True), (cm, False)):
        for side, src in ((0, fxm), (1, fxp)):
            base = side * CHALF
            for n, (d, e) in enumerate(TRI):
                b = NB - e if high else e - 1
                out[base + n] = src[XR + corner_row(side, d) * NB + b]
            tile = 3 if high else 0
            for i in range(H):
                out[base + CG + i] = src[XG + i * 4 + tile]
                out[base + CS + i] = src[XS + i * 4 + tile]
            out[base + CN] = src[XN]
            out[base + CN + 1] = src[XN + 1]


def widen(mid, left, right):
    lane = lax.broadcasted_iota(jnp.int32, (8, 128), 1)
    out = jnp.where((lane >= 8) & (lane < 40), pltpu.roll(mid, 8, 1), 0.0)
    if left is not None:
        out = jnp.where(lane < 8, pltpu.roll(left, 104, 1), out)
        moved = pltpu.roll(right, 40, 1)
        out = jnp.where((lane >= 40) & (lane < 48), moved, out)
    return out


def bounds():
    lane48 = lax.broadcasted_iota(jnp.int32, (QB, 128), 1)
    return lane48, lane48 > 0, lane48 < NZ - 1


def around(ref, a, c):
    _, low48, high48 = bounds()
    s = ref[a - 1] + ref[a + 1]
    s = s + pltpu.roll(c, 1, 0) + pltpu.roll(c, QB - 1, 0)
    s = s + jnp.where(low48, pltpu.roll(c, 1, 1), 0.0)
    return s + jnp.where(high48, pltpu.roll(c, NZ - 1, 1), 0.0)


def ground(gs, gt, fn, en, rows, gnd, fx=None, fy=None, cy=None):
    nothing = (None, None)
    for q in range(2):
        gs[q] = jnp.zeros((128, 128), f32)
        if fx is not None:
            sides = nothing if cy is None else [c[CN + q] for c in cy]
            gs[q, 0:8, :] = widen(fx[0][XN + q], *sides)
        for t in range(2):
            sides = nothing if fy is None else [f[YN + 2 * q + t] for f in fy]
            gs[q, H + 8 * t : H + 8 * t + 8, :] = widen(gnd[2 * q + t], *sides)
        if fx is not None:
            sides = nothing if cy is None else [c[CHALF + CN + q] for c in cy]
            gs[q, H + NA : H + NA + 8, :] = widen(fx[1][XN + q], *sides)
        gt[q, :, 0:32] = gs[q, 0:32, :].T
    lane48, low48, high48 = bounds()
    for a in rows:
        g = jnp.broadcast_to(gt[0, 0:QB, a : a + 1], (QB, 128))
        c = jnp.broadcast_to(gt[1, 0:QB, a : a + 1], (QB, 128))
        fn[a] = jnp.where(lane48.astype(f32) >= NZ - g, 1.0, 0.0)
        bottom = jnp.where(c == 1.0, 0.5, jnp.where(c == 2.0, 2.0, 0.0))
        en[a] = jnp.where(low48, 0.0, bottom) + jnp.where(high48, 0.0, 1.0)


def coefficients(fn, en, em, lo, hi, columns):
    def one(a):
        fluid = fn[a]
        e = jnp.where(fluid > 0.0, (CENTER - around(fn, a, fluid) - en[a]) * TWO, DRY)
        en[a] = e
        for b in columns:
            em[a, b] = jnp.broadcast_to(e[b + 1 : b + 2, :], (8, 128))

    count = (hi - lo) // 4

    def body(i, carry):
        for n in range(4):
            one(lo + i * 4 + n)
        return carry

    lax.fori_loop(0, count, body, 0)
    for a in range(lo + count * 4, hi):
        one(a)


def flags(fn, em, a, columns):
    f = jnp.where(fn[a] > 0.0, 0.0, DRY)
    for b in columns:
        em[a, b] = jnp.broadcast_to(f[b + 1 : b + 2, :], (8, 128))


def keep(ua, em, a, b, value):
    ua[a, b] = jnp.where(em[a, b] > 0.5 * DRY, value, 0.0)


def sweep(level, src, dst, em, tm, lo_a, hi_a, spans, more, unroll):
    lane = lax.broadcasted_iota(jnp.int32, (8, 128), 1)
    low8, high8 = lane > 0, lane < NZ - 1

    def row(a, own):
        for lo_b, hi_b in spans:
            before, here = src[a, lo_b - 1], src[a, lo_b]
            for b in range(lo_b, hi_b):
                after = src[a, b + 1]
                s = (src[a - 1, b] + src[a + 1, b]) + (before + after)
                s = s + jnp.where(low8, pltpu.roll(here, 1, 1), 0.0)
                s = s + jnp.where(high8, pltpu.roll(here, NZ - 1, 1), 0.0)
                e = em[a, b]
                two = jnp.where(e > 0.5 * DRY, e * here + TWO * s, 0.0)
                if level == 0:
                    out = CENTER * here - (0.5 * HALF) * two
                elif level == 1:
                    out = 0.5 * two
                else:
                    out = two - dst[a, b]
                dst[a, b] = out
                if own and H <= b < H + NB:
                    tm[level, a - H, b - H] = out
                before, here = here, after
        if more is not None:
            more(a, own)

    for lo, hi, own in ((lo_a, H, False), (H, H + NA, True), (H + NA, hi_a, False)):
        lo, hi = max(lo, lo_a), min(hi, hi_a)
        count = max(hi - lo, 0) // unroll

        def body(i, carry, lo=lo, own=own):
            for n in range(unroll):
                row(lo + i * unroll + n, own)
            return carry

        if count:
            lax.fori_loop(0, count, body, 0)
        for a in range(lo + count * unroll, hi):
            row(a, own)


def levels(ua, ub, em, tm, region, more=None, unroll=4):
    for level in range(7):
        src, dst = (ua, ub) if level % 2 == 0 else (ub, ua)
        for lo_a, hi_a, spans in region(level):
            extra = None if more is None else more(level)
            sweep(level, src, dst, em, tm, lo_a, hi_a, spans, extra, unroll)


def inner_kernel(rm, gnd, ua, ub, em, tm, gs, gt, fn, en):
    first, last, left, right = H, H + NA - 1, H, H + NB - 1
    ground(gs, gt, fn, en, range(first, last + 1), gnd)
    coefficients(fn, en, em, first + 1, last, range(left + 1, right))
    for a in (first, last):
        flags(fn, em, a, range(left, right + 1))
    for a in range(first + 1, last):
        flags(fn, em, a, (left, right))

    def own(a, carry):
        for b in range(NB):
            keep(ua, em, H + a, H + b, rm[a, b])
        return carry

    lax.fori_loop(0, NA, own, 0)
    levels(ua, ub, em, tm, lambda j: [(8 + j, 22 - j, [(8 + j, 38 - j)])])


def strip_kernel(gnd, fxm, fxp, _a, _b, _e, _t, ua, ub, em, tm, gs, gt, fn, en):
    rows = (*range(H + 2), *range(H + NA - 2, PA))
    ground(gs, gt, fn, en, rows, gnd, (fxm, fxp))
    inside = range(H + 1, H + NB - 1)
    coefficients(fn, en, em, 1, H + 1, inside)
    coefficients(fn, en, em, H + NA - 1, PA - 1, inside)
    for a in (0, PA - 1):
        flags(fn, em, a, range(H, H + NB))
    for a in (*range(1, H), *range(H + NA, PA - 1)):
        flags(fn, em, a, (H, H + NB - 1))
    for top, src in ((0, fxm), (H + NA, fxp)):

        def rows(i, carry, src=src, top=top):
            for b in range(NB):
                keep(ua, em, top + i, H + b, src[XR + i * NB + b])
            return carry

        lax.fori_loop(0, H, rows, 0)

    def region(j):
        spans = [(8 + j, 38 - j)]
        return [(1 + j, 8 + j, spans), (22 - j, 29 - j, spans)]

    levels(ua, ub, em, tm, region)


def main_kernel(
    rm, guess, right, gnd, fxm, fxp, fym, fyp, cym, cyp, _a, _b, _e, _t,
    pay, tr, rs, fo, ua, ub, em, tm,
    fn, en, va, vb, gs, gt, flat,
):
    lane = lax.broadcasted_iota(jnp.int32, (8, 128), 1)
    sub = lax.broadcasted_iota(jnp.int32, (8, 128), 0)
    ground(gs, gt, fn, en, range(PA), gnd, (fxm, fxp), (fym, fyp), (cym, cyp))
    rim = (*range(1, H + 1), *range(H + NB - 1, PB - 1))
    coefficients(fn, en, em, 1, PA - 1, rim)
    for a in (0, PA - 1):
        flags(fn, em, a, (*range(0, H), *range(H + NB, PB)))

    def ends(a, carry):
        flags(fn, em, a, (0, PB - 1))
        return carry

    lax.fori_loop(1, PA - 1, ends, 0)

    zero8 = jnp.zeros((8, 128), f32)
    for i in range(H):
        for b in range(H):
            for a in (i, H + NA + i):
                ua[a, b] = zero8
                ua[a, H + NB + b] = zero8
    for side in range(2):
        top = 0 if side == 0 else H + NA
        for n, (d, e) in enumerate(TRI):
            a = top + corner_row(side, d)
            keep(ua, em, a, H - e, cym[side * CHALF + n])
            keep(ua, em, a, H + NB + e - 1, cyp[side * CHALF + n])

    def sides(a, carry):
        for i in range(H):
            keep(ua, em, H + a, i, fym[YR + a * H + i])
            keep(ua, em, H + a, H + NB + i, fyp[YR + a * H + i])
        return carry

    lax.fori_loop(0, NA, sides, 0)

    for ref, mid, xo, yo, co in ((va, guess, XG, YG, CG), (vb, right, XS, YS, CS)):
        for a in range(NA):
            ref[H + a, 8:40, :] = mid[a]
            ref[H + a, 0:8, :] = fym[yo + a]
            ref[H + a, 40:48, :] = fyp[yo + a]
        for side, src in ((0, fxm), (1, fxp)):
            top = 0 if side == 0 else H + NA
            for i in range(H):
                for t in range(4):
                    ref[top + i, 8 + 8 * t : 16 + 8 * t, :] = src[xo + 4 * i + t]
                ref[top + i, 0:8, :] = cym[side * CHALF + co + i]
                ref[top + i, 40:48, :] = cyp[side * CHALF + co + i]
    for a in range(NA):
        f = fn[H + a, 8:40, :]
        fo[a] = f
        rs[a] = jnp.where(f > 0.0, 0.0, right[a] - guess[a])
    for a in range(PA):
        wet = fn[a] > 0.0
        va[a] = jnp.where(wet, va[a], 0.0)
        vb[a] = jnp.where(wet, vb[a], 0.0)

    def single(level):
        vsrc, vdst = (va, vb) if level % 2 == 0 else (vb, va)

        def row_of(a, own):
            c = vsrc[a]
            two = en[a] * c + fn[a] * TWO * around(vsrc, a, c)
            if level == 0:
                out = vdst[a] - (CENTER * c - (0.5 * HALF) * two)
            elif level == 1:
                out = 0.5 * two
            else:
                out = two - vdst[a]
            vdst[a] = out
            if own:
                tr[level, a - H] = out[8:40, :]

        return row_of

    def region(j):
        return [(1 + j, 29 - j, [(1 + j, 8 + j), (38 - j, 45 - j)])]

    levels(ua, ub, em, tm, region, single, 8)

    def joined(ref, at, dry):
        base = ref[(0, *at)]
        return (
            base + dry,
            ref[(3, *at)] + TS[3] * dry,
            (ref[(6, *at)] + base) + (TS[6] + 1.0) * dry,
        )

    def gather(i, carry):
        grams, cross, powers = carry
        a, t = i // 4, i % 4
        rows = pl.ds(t * 8, 8)
        r0, r3, r6 = joined(tr, (a, rows), rs[a, rows, :])
        pairs = (r0 * r0, r0 * r3, r0 * r6, r3 * r6, r6 * r6)
        powers = [p + v for p, v in zip(powers, pairs)]
        for n, value in enumerate((r0, r3, r6)):
            flat[n] = value
        for q in range(8):
            b = t * 8 + q
            dry = jnp.where(em[H + a, H + b] > 0.5 * DRY, 0.0, rm[a, b])
            t0, t3, t6 = joined(tm, (a, b), dry)
            new = [list(g) for g in grams]
            for k in range(5):
                v0 = t0 if k == 0 else pltpu.roll(t0, k, 0)
                v6 = t6 if k == 0 else pltpu.roll(t6, k, 0)
                for n, v in enumerate((t0 * v0, t3 * v0, t6 * v0, t3 * v6, t6 * v6)):
                    new[n][k] = new[n][k] + v
            grams = new
            w0, w3, w6 = [flat[n, pl.ds(q, 8, stride=0), :] for n in range(3)]
            pairs = (t0 * w0, t0 * w3, t0 * w6, t3 * w6, t6 * w6)
            cross = [c + v for c, v in zip(cross, pairs)]
        return grams, cross, powers

    five = [zero8] * 5
    grams, cross, powers = lax.fori_loop(0, NA * 4, gather, ([five] * 5, five, five))
    scale = (1.0, E3, 0.5 * E3**2, 0.5 * E3**3, 0.25 * E3**4)
    packed = zero8
    for k in range(5):
        for r in range(5):
            value = scale[k] * jnp.sum(grams[k][r], axis=1, keepdims=True)
            packed = jnp.where(lane == 5 * k + r, value, packed)
        value = scale[k] * jnp.sum(cross[k], axis=1, keepdims=True)
        packed = jnp.where(lane == 25 + k, value, packed)
        value = scale[k] * jnp.sum(powers[k], axis=1, keepdims=True)
        value = jnp.sum(value, axis=0, keepdims=True)
        packed = jnp.where((lane == 30) & (sub == k), value, packed)
    packed = jnp.where(lane < 32, packed, 0.0)
    quarter = sub % 4
    moved = packed
    for i in range(1, 4):
        moved = jnp.where(quarter == i, pltpu.roll(packed, 32 * i, 1), moved)
    upper = jnp.sum(jnp.where(sub < 4, moved, 0.0), axis=0, keepdims=True)
    lower = jnp.sum(jnp.where(sub < 4, 0.0, moved), axis=0, keepdims=True)
    both = jnp.concatenate([upper, lower], axis=0)
    pay[...] = jnp.broadcast_to(both[None], pay.shape)


def tail_kernel(got, rm, guess, tm, tr, rs, fo, out_x, out_r):
    lane = lax.broadcasted_iota(jnp.int32, (8, 128), 1)
    sub = lax.broadcasted_iota(jnp.int32, (8, 128), 0)
    total = jnp.sum(got[...], axis=0)
    spread = jnp.where(
        sub < 4,
        jnp.broadcast_to(total[0:1, :], (8, 128)),
        jnp.broadcast_to(total[1:2, :], (8, 128)),
    )
    quarter = sub % 4
    packed = spread
    for i in range(1, 4):
        packed = jnp.where(quarter == i, pltpu.roll(spread, 128 - 32 * i, 1), packed)

    def column(j):
        return jnp.broadcast_to(packed[:, j : j + 1], (8, 128))

    def over_m(v):
        return jnp.broadcast_to(jnp.sum(v, axis=0, keepdims=True), (8, 128))

    diag = [[column(5 * k + r) for r in range(5)] for k in range(5)]
    cross = [column(25 + k) for k in range(5)]
    powers = column(30)
    rho = [over_m(jnp.where(sub == k, powers, 0.0)) for k in range(5)]

    def times(k, v):
        out = diag[k][0] * v
        for r in range(1, 5):
            out = out + diag[k][r] * pltpu.roll(v, r, 0)
        for r in range(1, 4):
            out = out + pltpu.roll(diag[k][r] * v, 8 - r, 0)
        return out

    mat = jnp.where(lane == sub + 8, 1.0, 0.0)
    for r in range(5):
        mat = jnp.where(lane == (sub + 8 - r) % 8, diag[0][r], mat)
    for r in range(1, 4):
        mat = jnp.where(lane == (sub + r) % 8, pltpu.roll(diag[0][r], 8 - r, 0), mat)
    for k in range(8):
        pivot_row = jnp.broadcast_to(mat[k : k + 1, :], (8, 128))
        pivot_row = pivot_row / jnp.broadcast_to(pivot_row[:, k : k + 1], (8, 128))
        factor = jnp.broadcast_to(mat[:, k : k + 1], (8, 128))
        mat = jnp.where(sub == k, pivot_row, mat - factor * pivot_row)
    inverse = jnp.where((lane >= 8) & (lane < 16), mat, 0.0)

    def solve(v):
        flat = over_m(jnp.where(lane == sub + 8, v, 0.0))
        return jnp.broadcast_to(
            jnp.sum(inverse * flat, axis=1, keepdims=True), (8, 128)
        )

    def apply(k, v):
        return times(k, v[0]) + cross[k] * v[1], over_m(cross[k] * v[0]) + rho[k] * v[1]

    def dot(u, v):
        return over_m(u[0] * v[0]) + u[1] * v[1]

    coeffs = solve(cross[0])
    one = jnp.ones((8, 128), f32)
    a = (-coeffs, one)
    n0, n1, n2 = apply(0, a), apply(1, a), apply(2, a)
    g = n0[0] - n1[0]
    y1 = solve(g)
    rr, re, ee = dot(a, n0), dot(a, n1), dot(a, n2)
    s1 = (rr - re - over_m(y1 * n0[0])) / (rr - 2.0 * re + ee - over_m(y1 * g))
    a0 = ((1.0 - s1) * a[0] + s1 * y1, (1.0 - s1) * a[1])
    a1 = (s1 * a[0], s1 * a[1])
    m0, m1, m2, m3 = apply(0, a0), apply(1, a0), apply(2, a0), apply(3, a0)
    l3, l4 = apply(3, a1), apply(4, a1)
    h = m0[0] + s1 * n1[0]
    g = h - (m1[0] + s1 * n2[0])
    y2 = solve(g)
    rr = dot(a0, m0) + 2.0 * dot(a1, m1) + s1 * dot(a1, n2)
    re = dot(a0, m1) + 2.0 * dot(a1, m2) + dot(a1, l3)
    ee = dot(a0, m2) + 2.0 * dot(a1, m3) + dot(a1, l4)
    s2 = (rr - re - over_m(y2 * h)) / (rr - 2.0 * re + ee - over_m(y2 * g))

    half = 0.5 * E3 * E3
    weights_r, weights_x = [], []
    for i in range(2):
        extra = s2 * y2 if i == 0 else 0.0
        weights_r.append((
            (1.0 - s2) * a0[i] + extra + half * s2 * a1[i],
            E3 * ((1.0 - s2) * a1[i] + s2 * a0[i]),
            half * s2 * a1[i],
        ))
        d0 = s1 * a[i] + s2 * a0[i]
        d1 = E3 * s2 * a1[i]
        weights_x.append((
            P0 * d0,
            P1 * d0 + (0.5 * P2) * d1,
            P2 * d0 + (0.5 * P1) * d1,
            P0 * d1,
            (0.5 * P1) * d1,
            (0.5 * P2) * d1,
        ))
    direct = coeffs - s1 * y1 - s2 * y2
    levels_r = (0, 3, 6)
    solid_r = [sum(w * TS[j] for w, j in zip(ws, levels_r)) for ws in weights_r]
    solid_x = [sum(w * TS[j] for j, w in enumerate(ws)) for ws in weights_x]

    odd = [(sub // step) % 2 == 1 for step in (1, 2, 4)]

    def each_over_m(values):
        for n, step in enumerate((1, 2, 4)):
            merged = []
            for u, v in zip(values[0::2], values[1::2]):
                stay, move = jnp.where(odd[n], v, u), jnp.where(odd[n], u, v)
                merged.append(stay + pltpu.roll(move, step, 0))
            values = merged
        return values[0]

    def tile(i):
        p, t = i // 4, i % 4
        rows = pl.ds(t * 8, 8)
        ff = fo[p, rows, :]
        base_x = guess[p, rows, :]
        parts_x, parts_r = [], []
        for q in range(8):
            b = t * 8 + q
            r = rm[p, b]
            dry = jnp.where(jnp.broadcast_to(ff[q : q + 1, :], (8, 128)) > 0.0, 0.0, r)
            us = [tm[j, p, b] for j in range(7)]
            vx = direct * r + solid_x[0] * dry
            for j in range(6):
                vx = vx + weights_x[0][j] * us[j]
            vr = solid_r[0] * dry
            for w, j in zip(weights_r[0], levels_r):
                vr = vr + w * us[j]
            parts_x.append(vx)
            parts_r.append(vr)
        base_x = base_x + each_over_m(parts_x)
        base_r = each_over_m(parts_r)
        dry = rs[p, rows, :]
        vs = [tr[j, p, rows, :] for j in range(7)]
        base_x = base_x + solid_x[1] * dry
        base_r = base_r + solid_r[1] * dry
        for j in range(6):
            base_x = base_x + weights_x[1][j] * vs[j]
        for w, j in zip(weights_r[1], levels_r):
            base_r = base_r + w * vs[j]
        out_x[p, rows, :] = base_x
        out_r[p, rows, :] = base_r

    def tiles(i, carry):
        tile(2 * i)
        tile(2 * i + 1)
        return carry

    lax.fori_loop(0, NA * 2, tiles, 0)


def call(kernel, outs, scratch, limit, *args, aliases=None, cost=None):
    return pl.pallas_call(
        kernel,
        out_shape=tuple(jax.ShapeDtypeStruct(s, f32) for s in outs),
        in_specs=[VMEM] * len(args),
        out_specs=tuple([VMEM] * len(outs)),
        scratch_shapes=[pltpu.VMEM(s, f32) for s in scratch],
        input_output_aliases=aliases or {},
        cost_estimate=cost,
        compiler_params=pltpu.CompilerParams(vmem_limit_bytes=limit),
    )(*args)


def local(right_side, first_guess, recycled, heights, ground_codes):
    mib = 1 << 20
    long = pl.CostEstimate(flops=10**10, bytes_accessed=4 * 10**7, transcendentals=0)
    faces = ((XTILES, 8, 128), (XTILES, 8, 128), (YTILES, 8, 128), (YTILES, 8, 128))
    rm, *sends = call(
        vectors_kernel, ((NA * NB * K, 128), *faces), (), 4 * mib, recycled, cost=long
    )
    gnd, sxp, sxm, syp, sym = call(
        rest_kernel, ((4, 8, 128), *faces), (), 4 * mib,
        first_guess, right_side, heights, ground_codes, *sends,
        aliases={4: 1, 5: 2, 6: 3, 7: 4},
    )
    rm = rm.reshape(NA, NB, K, 128)

    def shift(value, axis, way):
        size = lax.axis_size(axis)
        pairs = [(i, i + way) for i in range(size) if 0 <= i + way < size]
        return lax.ppermute(value, axis, pairs)

    wide, flat = (PA, PB, 8, 128), (PA, QB, 128)
    fields = (wide, wide, wide, (7, NA, NB, 8, 128))
    small = ((2, 128, 128), (2, 128, 128), flat, flat)
    fxm, fxp = shift(sxp, "gx", 1), shift(sxm, "gx", -1)
    fym, fyp = shift(syp, "gy", 1), shift(sym, "gy", -1)
    state = call(inner_kernel, fields, small, 8 * mib, rm, gnd, cost=long)
    cp, cm = call(
        corner_kernel, ((CTILES, 8, 128), (CTILES, 8, 128)), (), 8 * mib, fxm, fxp
    )
    cym, cyp = shift(cp, "gy", 1), shift(cm, "gy", -1)
    state = call(
        strip_kernel, fields, small, 8 * mib, gnd, fxm, fxp, *state,
        aliases={3: 0, 4: 1, 5: 2, 6: 3}, cost=long,
    )
    pay, tr, rs, fo, _, _, _, tm = call(
        main_kernel,
        ((256, 2, 128), (7, NA, NB, 128), (NA, NB, 128), (NA, NB, 128), *fields),
        (flat, flat, flat, flat, (2, 128, 128), (2, 128, 128), (3, 8, 128)),
        8 * mib,
        rm, first_guess, right_side, gnd, fxm, fxp, fym, fyp, cym, cyp, *state,
        aliases={10: 4, 11: 5, 12: 6, 13: 7},
    )
    got = lax.all_to_all(pay, ("gx", "gy"), 0, 0)
    return call(
        tail_kernel,
        ((NA, NB, 128), (NA, NB, 128)),
        (),
        8 * mib,
        got, rm, first_guess, tm, tr, rs, fo,
    )


def solution(mesh):
    placed = (
        P("gx", "gy", None),
        P("gx", "gy", None),
        P(None, "gx", "gy", None),
        P("gx", "gy"),
        P("gx", "gy"),
    )
    return jax.shard_map(
        local,
        mesh=mesh,
        in_specs=placed,
        out_specs=(P("gx", "gy", None), P("gx", "gy", None)),
        check_vma=False,
    )
```

```python
import jax
import jax.numpy as jnp
from jax import lax
from jax.experimental import pallas as pl
from jax.experimental.pallas import tpu as pltpu
from jax.sharding import PartitionSpec as P

NZ = 128
K = 8
H = 7
NA = 16
NB = 32
PA = NA + 2 * H
PB = NB + 2 * H
QB = NB + 16

CENTER = 7.25
HALF = 6.75
SIGMA = CENTER / HALF
T3 = 4.0 * SIGMA**3 - 3.0 * SIGMA
E3 = 1.0 / T3
TWO = 2.0 / HALF
DRY = -100.0
SOLID = (CENTER - 1.0) / HALF
TS = [1.0, SOLID]
for _ in range(5):
    TS.append(2.0 * SOLID * TS[-1] - TS[-2])
P0 = (4.0 * SIGMA**2 - 1.0) / (HALF * T3)
P1 = 4.0 * SIGMA / (HALF * T3)
P2 = 2.0 / (HALF * T3)

XR, XG, XS, XN = 0, 224, 252, 280
XTILES = 282
YR, YG, YS, YN = 0, 112, 128, 144
YTILES = 148
TRI = [(d, e) for d in range(1, H) for e in range(1, H + 1 - d)]
CG, CS, CN = len(TRI), len(TRI) + 7, len(TRI) + 14
CHALF = len(TRI) + 16
CTILES = 2 * CHALF

f32 = jnp.float32
VMEM = pl.BlockSpec(memory_space=pltpu.VMEM)


def vectors_kernel(rec, rm, sxp, sxm, syp, sym):
    for m in range(K):

        def body(a, carry, m=m):
            rm[pl.ds(a * (NB * K) + m, NB, stride=K), :] = rec[m, a].astype(f32)
            return carry

        lax.fori_loop(0, NA, body, 0)
    for out, lo in ((sxp, NA - H), (sxm, 0)):
        for i in range(H):
            for b in range(NB):
                at = ((lo + i) * NB + b) * K
                out[XR + i * NB + b] = rm[at : at + K, :]
    for out, lo in ((syp, NB - H), (sym, 0)):
        for a in range(NA):
            for i in range(H):
                at = (a * NB + lo + i) * K
                out[YR + a * H + i] = rm[at : at + K, :]


def rest_kernel(guess, right, heights, codes, _p, _m, _q, _n, gnd, sxp, sxm, syp, sym):
    for t in range(4):
        gnd[t] = jnp.zeros((8, 128), f32)
    for t in range(2):
        gnd[t, :, 0:NB] = (NZ - heights[8 * t : 8 * t + 8, :]).astype(f32)
        gnd[2 + t, :, 0:NB] = codes[8 * t : 8 * t + 8, :].astype(f32)
    for out, lo in ((sxp, NA - H), (sxm, 0)):
        for i in range(H):
            for t in range(4):
                out[XG + i * 4 + t] = guess[lo + i, 8 * t : 8 * t + 8, :]
                out[XS + i * 4 + t] = right[lo + i, 8 * t : 8 * t + 8, :]
        for t in range(2):
            out[XN + t] = jnp.zeros((8, 128), f32)
        out[XN, 0:H, 0:NB] = (NZ - heights[lo : lo + H, :]).astype(f32)
        out[XN + 1, 0:H, 0:NB] = codes[lo : lo + H, :].astype(f32)
    for out, tile in ((syp, 3), (sym, 0)):
        for a in range(NA):
            out[YG + a] = guess[a, 8 * tile : 8 * tile + 8, :]
            out[YS + a] = right[a, 8 * tile : 8 * tile + 8, :]
        for t in range(4):
            out[YN + t] = gnd[t]


def corner_row(side, d):
    return H - d if side == 0 else d - 1


def corner_kernel(fxm, fxp, cp, cm):
    for out, high in ((cp, True), (cm, False)):
        for side, src in ((0, fxm), (1, fxp)):
            base = side * CHALF
            for n, (d, e) in enumerate(TRI):
                b = NB - e if high else e - 1
                out[base + n] = src[XR + corner_row(side, d) * NB + b]
            tile = 3 if high else 0
            for i in range(H):
                out[base + CG + i] = src[XG + i * 4 + tile]
                out[base + CS + i] = src[XS + i * 4 + tile]
            out[base + CN] = src[XN]
            out[base + CN + 1] = src[XN + 1]


def widen(mid, left, right):
    lane = lax.broadcasted_iota(jnp.int32, (8, 128), 1)
    out = jnp.where((lane >= 8) & (lane < 40), pltpu.roll(mid, 8, 1), 0.0)
    if left is not None:
        out = jnp.where(lane < 8, pltpu.roll(left, 104, 1), out)
        moved = pltpu.roll(right, 40, 1)
        out = jnp.where((lane >= 40) & (lane < 48), moved, out)
    return out


def bounds():
    lane48 = lax.broadcasted_iota(jnp.int32, (QB, 128), 1)
    return lane48, lane48 > 0, lane48 < NZ - 1


def around(ref, a, c):
    _, low48, high48 = bounds()
    s = ref[a - 1] + ref[a + 1]
    s = s + pltpu.roll(c, 1, 0) + pltpu.roll(c, QB - 1, 0)
    s = s + jnp.where(low48, pltpu.roll(c, 1, 1), 0.0)
    return s + jnp.where(high48, pltpu.roll(c, NZ - 1, 1), 0.0)


def ground(gs, gt, fn, en, rows, gnd, fx=None, fy=None, cy=None):
    nothing = (None, None)
    for q in range(2):
        gs[q] = jnp.zeros((128, 128), f32)
        if fx is not None:
            sides = nothing if cy is None else [c[CN + q] for c in cy]
            gs[q, 0:8, :] = widen(fx[0][XN + q], *sides)
        for t in range(2):
            sides = nothing if fy is None else [f[YN + 2 * q + t] for f in fy]
            gs[q, H + 8 * t : H + 8 * t + 8, :] = widen(gnd[2 * q + t], *sides)
        if fx is not None:
            sides = nothing if cy is None else [c[CHALF + CN + q] for c in cy]
            gs[q, H + NA : H + NA + 8, :] = widen(fx[1][XN + q], *sides)
        gt[q, :, 0:32] = gs[q, 0:32, :].T
    lane48, low48, high48 = bounds()
    for a in rows:
        g = jnp.broadcast_to(gt[0, 0:QB, a : a + 1], (QB, 128))
        c = jnp.broadcast_to(gt[1, 0:QB, a : a + 1], (QB, 128))
        fn[a] = jnp.where(lane48.astype(f32) >= NZ - g, 1.0, 0.0)
        bottom = jnp.where(c == 1.0, 0.5, jnp.where(c == 2.0, 2.0, 0.0))
        en[a] = jnp.where(low48, 0.0, bottom) + jnp.where(high48, 0.0, 1.0)


def coefficients(fn, en, em, lo, hi, columns):
    def one(a):
        fluid = fn[a]
        e = jnp.where(fluid > 0.0, (CENTER - around(fn, a, fluid) - en[a]) * TWO, DRY)
        en[a] = e
        for b in columns:
            em[a, b] = jnp.broadcast_to(e[b + 1 : b + 2, :], (8, 128))

    count = (hi - lo) // 7

    def body(i, carry):
        for n in range(7):
            one(lo + i * 7 + n)
        return carry

    lax.fori_loop(0, count, body, 0)
    for a in range(lo + count * 7, hi):
        one(a)


def flags(fn, em, a, columns):
    f = jnp.where(fn[a] > 0.0, 0.0, DRY)
    for b in columns:
        em[a, b] = jnp.broadcast_to(f[b + 1 : b + 2, :], (8, 128))


def keep(ua, em, a, b, value):
    ua[a, b] = jnp.where(em[a, b] > 0.5 * DRY, value, 0.0)


def sweep(level, src, dst, em, tm, lo_a, hi_a, spans, more, unroll):
    lane = lax.broadcasted_iota(jnp.int32, (8, 128), 1)
    low8, high8 = lane > 0, lane < NZ - 1

    def row(a, own):
        for lo_b, hi_b in spans:
            before, here = src[a, lo_b - 1], src[a, lo_b]
            for b in range(lo_b, hi_b):
                after = src[a, b + 1]
                s = (src[a - 1, b] + src[a + 1, b]) + (before + after)
                s = s + jnp.where(low8, pltpu.roll(here, 1, 1), 0.0)
                s = s + jnp.where(high8, pltpu.roll(here, NZ - 1, 1), 0.0)
                e = em[a, b]
                two = jnp.where(e > 0.5 * DRY, e * here + TWO * s, 0.0)
                if level == 0:
                    out = CENTER * here - (0.5 * HALF) * two
                elif level == 1:
                    out = 0.5 * two
                else:
                    out = two - dst[a, b]
                dst[a, b] = out
                if own and H <= b < H + NB:
                    tm[level, a - H, b - H] = out
                before, here = here, after
        if more is not None:
            more(a, own)

    for lo, hi, own in ((lo_a, H, False), (H, H + NA, True), (H + NA, hi_a, False)):
        lo, hi = max(lo, lo_a), min(hi, hi_a)
        count = max(hi - lo, 0) // unroll

        def body(i, carry, lo=lo, own=own):
            for n in range(unroll):
                row(lo + i * unroll + n, own)
            return carry

        if count:
            lax.fori_loop(0, count, body, 0)
        for a in range(lo + count * unroll, hi):
            row(a, own)


def levels(ua, ub, em, tm, region, more=None, unroll=4):
    for level in range(7):
        src, dst = (ua, ub) if level % 2 == 0 else (ub, ua)
        for lo_a, hi_a, spans in region(level):
            extra = None if more is None else more(level)
            sweep(level, src, dst, em, tm, lo_a, hi_a, spans, extra, unroll)


def inner_kernel(rm, gnd, ua, ub, em, tm, gs, gt, fn, en):
    first, last, left, right = H, H + NA - 1, H, H + NB - 1
    ground(gs, gt, fn, en, range(first, last + 1), gnd)
    coefficients(fn, en, em, first + 1, last, range(left + 1, right))
    for a in (first, last):
        flags(fn, em, a, range(left, right + 1))
    for a in range(first + 1, last):
        flags(fn, em, a, (left, right))

    def own(a, carry):
        for b in range(NB):
            keep(ua, em, H + a, H + b, rm[a, b])
        return carry

    lax.fori_loop(0, NA, own, 0)
    levels(ua, ub, em, tm, lambda j: [(8 + j, 22 - j, [(8 + j, 38 - j)])])


def strip_kernel(gnd, fxm, fxp, _a, _b, _e, _t, ua, ub, em, tm, gs, gt, fn, en):
    rows = (*range(H + 2), *range(H + NA - 2, PA))
    ground(gs, gt, fn, en, rows, gnd, (fxm, fxp))
    inside = range(H + 1, H + NB - 1)
    coefficients(fn, en, em, 1, H + 1, inside)
    coefficients(fn, en, em, H + NA - 1, PA - 1, inside)
    for a in (0, PA - 1):
        flags(fn, em, a, range(H, H + NB))
    for a in (*range(1, H), *range(H + NA, PA - 1)):
        flags(fn, em, a, (H, H + NB - 1))
    for top, src in ((0, fxm), (H + NA, fxp)):

        def rows(i, carry, src=src, top=top):
            for b in range(NB):
                keep(ua, em, top + i, H + b, src[XR + i * NB + b])
            return carry

        lax.fori_loop(0, H, rows, 0)

    def region(j):
        spans = [(8 + j, 38 - j)]
        return [(1 + j, 8 + j, spans), (22 - j, 29 - j, spans)]

    levels(ua, ub, em, tm, region)


def main_kernel(
    rm, guess, right, gnd, fxm, fxp, fym, fyp, cym, cyp, _a, _b, _e, _t,
    pay, tr, rs, fo, ua, ub, em, tm,
    fn, en, va, vb, gs, gt, flat,
):
    lane = lax.broadcasted_iota(jnp.int32, (8, 128), 1)
    sub = lax.broadcasted_iota(jnp.int32, (8, 128), 0)
    ground(gs, gt, fn, en, range(PA), gnd, (fxm, fxp), (fym, fyp), (cym, cyp))
    rim = (*range(1, H + 1), *range(H + NB - 1, PB - 1))
    coefficients(fn, en, em, 1, PA - 1, rim)
    for a in (0, PA - 1):
        flags(fn, em, a, (*range(0, H), *range(H + NB, PB)))

    def ends(a, carry):
        flags(fn, em, a, (0, PB - 1))
        return carry

    lax.fori_loop(1, PA - 1, ends, 0)

    zero8 = jnp.zeros((8, 128), f32)
    for i in range(H):
        for b in range(H):
            for a in (i, H + NA + i):
                ua[a, b] = zero8
                ua[a, H + NB + b] = zero8
    for side in range(2):
        top = 0 if side == 0 else H + NA
        for n, (d, e) in enumerate(TRI):
            a = top + corner_row(side, d)
            keep(ua, em, a, H - e, cym[side * CHALF + n])
            keep(ua, em, a, H + NB + e - 1, cyp[side * CHALF + n])

    def sides(a, carry):
        for i in range(H):
            keep(ua, em, H + a, i, fym[YR + a * H + i])
            keep(ua, em, H + a, H + NB + i, fyp[YR + a * H + i])
        return carry

    lax.fori_loop(0, NA, sides, 0)

    for ref, mid, xo, yo, co in ((va, guess, XG, YG, CG), (vb, right, XS, YS, CS)):
        for a in range(NA):
            ref[H + a, 8:40, :] = mid[a]
            ref[H + a, 0:8, :] = fym[yo + a]
            ref[H + a, 40:48, :] = fyp[yo + a]
        for side, src in ((0, fxm), (1, fxp)):
            top = 0 if side == 0 else H + NA
            for i in range(H):
                for t in range(4):
                    ref[top + i, 8 + 8 * t : 16 + 8 * t, :] = src[xo + 4 * i + t]
                ref[top + i, 0:8, :] = cym[side * CHALF + co + i]
                ref[top + i, 40:48, :] = cyp[side * CHALF + co + i]
    for a in range(NA):
        f = fn[H + a, 8:40, :]
        fo[a] = f
        rs[a] = jnp.where(f > 0.0, 0.0, right[a] - guess[a])
    for a in range(PA):
        wet = fn[a] > 0.0
        va[a] = jnp.where(wet, va[a], 0.0)
        vb[a] = jnp.where(wet, vb[a], 0.0)

    def single(level):
        vsrc, vdst = (va, vb) if level % 2 == 0 else (vb, va)

        def row_of(a, own):
            c = vsrc[a]
            two = en[a] * c + fn[a] * TWO * around(vsrc, a, c)
            if level == 0:
                out = vdst[a] - (CENTER * c - (0.5 * HALF) * two)
            elif level == 1:
                out = 0.5 * two
            else:
                out = two - vdst[a]
            vdst[a] = out
            if own:
                tr[level, a - H] = out[8:40, :]

        return row_of

    def region(j):
        return [(1 + j, 29 - j, [(1 + j, 8 + j), (38 - j, 45 - j)])]

    levels(ua, ub, em, tm, region, single, 16)

    def joined(ref, at, dry):
        base = ref[(0, *at)]
        return (
            base + dry,
            ref[(3, *at)] + TS[3] * dry,
            (ref[(6, *at)] + base) + (TS[6] + 1.0) * dry,
        )

    def gather(i, carry):
        grams, cross, powers = carry
        a, t = i // 4, i % 4
        rows = pl.ds(t * 8, 8)
        r0, r3, r6 = joined(tr, (a, rows), rs[a, rows, :])
        pairs = (r0 * r0, r0 * r3, r0 * r6, r3 * r6, r6 * r6)
        powers = [p + v for p, v in zip(powers, pairs)]
        for n, value in enumerate((r0, r3, r6)):
            flat[n] = value
        for q in range(8):
            b = t * 8 + q
            dry = jnp.where(em[H + a, H + b] > 0.5 * DRY, 0.0, rm[a, b])
            t0, t3, t6 = joined(tm, (a, b), dry)
            new = [list(g) for g in grams]
            for k in range(5):
                v0 = t0 if k == 0 else pltpu.roll(t0, k, 0)
                v6 = t6 if k == 0 else pltpu.roll(t6, k, 0)
                for n, v in enumerate((t0 * v0, t3 * v0, t6 * v0, t3 * v6, t6 * v6)):
                    new[n][k] = new[n][k] + v
            grams = new
            w0, w3, w6 = [flat[n, pl.ds(q, 8, stride=0), :] for n in range(3)]
            pairs = (t0 * w0, t0 * w3, t0 * w6, t3 * w6, t6 * w6)
            cross = [c + v for c, v in zip(cross, pairs)]
        return grams, cross, powers

    five = [zero8] * 5
    grams, cross, powers = lax.fori_loop(0, NA * 4, gather, ([five] * 5, five, five))
    scale = (1.0, E3, 0.5 * E3**2, 0.5 * E3**3, 0.25 * E3**4)
    packed = zero8
    for k in range(5):
        for r in range(5):
            value = scale[k] * jnp.sum(grams[k][r], axis=1, keepdims=True)
            packed = jnp.where(lane == 5 * k + r, value, packed)
        value = scale[k] * jnp.sum(cross[k], axis=1, keepdims=True)
        packed = jnp.where(lane == 25 + k, value, packed)
        value = scale[k] * jnp.sum(powers[k], axis=1, keepdims=True)
        value = jnp.sum(value, axis=0, keepdims=True)
        packed = jnp.where((lane == 30) & (sub == k), value, packed)
    packed = jnp.where(lane < 32, packed, 0.0)
    quarter = sub % 4
    moved = packed
    for i in range(1, 4):
        moved = jnp.where(quarter == i, pltpu.roll(packed, 32 * i, 1), moved)
    upper = jnp.sum(jnp.where(sub < 4, moved, 0.0), axis=0, keepdims=True)
    lower = jnp.sum(jnp.where(sub < 4, 0.0, moved), axis=0, keepdims=True)
    both = jnp.concatenate([upper, lower], axis=0)
    pay[...] = jnp.broadcast_to(both[None], pay.shape)


def tail_kernel(got, rm, guess, tm, tr, rs, fo, out_x, out_r):
    lane = lax.broadcasted_iota(jnp.int32, (8, 128), 1)
    sub = lax.broadcasted_iota(jnp.int32, (8, 128), 0)
    total = jnp.sum(got[...], axis=0)
    spread = jnp.where(
        sub < 4,
        jnp.broadcast_to(total[0:1, :], (8, 128)),
        jnp.broadcast_to(total[1:2, :], (8, 128)),
    )
    quarter = sub % 4
    packed = spread
    for i in range(1, 4):
        packed = jnp.where(quarter == i, pltpu.roll(spread, 128 - 32 * i, 1), packed)

    def column(j):
        return jnp.broadcast_to(packed[:, j : j + 1], (8, 128))

    def over_m(v):
        return jnp.broadcast_to(jnp.sum(v, axis=0, keepdims=True), (8, 128))

    diag = [[column(5 * k + r) for r in range(5)] for k in range(5)]
    cross = [column(25 + k) for k in range(5)]
    powers = column(30)
    rho = [over_m(jnp.where(sub == k, powers, 0.0)) for k in range(5)]

    def times(k, v):
        out = diag[k][0] * v
        for r in range(1, 5):
            out = out + diag[k][r] * pltpu.roll(v, r, 0)
        for r in range(1, 4):
            out = out + pltpu.roll(diag[k][r] * v, 8 - r, 0)
        return out

    mat = jnp.where(lane == sub + 8, 1.0, 0.0)
    for r in range(5):
        mat = jnp.where(lane == (sub + 8 - r) % 8, diag[0][r], mat)
    for r in range(1, 4):
        mat = jnp.where(lane == (sub + r) % 8, pltpu.roll(diag[0][r], 8 - r, 0), mat)
    for k in range(8):
        pivot_row = jnp.broadcast_to(mat[k : k + 1, :], (8, 128))
        pivot_row = pivot_row / jnp.broadcast_to(pivot_row[:, k : k + 1], (8, 128))
        factor = jnp.broadcast_to(mat[:, k : k + 1], (8, 128))
        mat = jnp.where(sub == k, pivot_row, mat - factor * pivot_row)
    inverse = jnp.where((lane >= 8) & (lane < 16), mat, 0.0)

    def solve(v):
        flat = over_m(jnp.where(lane == sub + 8, v, 0.0))
        return jnp.broadcast_to(
            jnp.sum(inverse * flat, axis=1, keepdims=True), (8, 128)
        )

    def apply(k, v):
        return times(k, v[0]) + cross[k] * v[1], over_m(cross[k] * v[0]) + rho[k] * v[1]

    def dot(u, v):
        return over_m(u[0] * v[0]) + u[1] * v[1]

    coeffs = solve(cross[0])
    one = jnp.ones((8, 128), f32)
    a = (-coeffs, one)
    n0, n1, n2 = apply(0, a), apply(1, a), apply(2, a)
    g = n0[0] - n1[0]
    y1 = solve(g)
    rr, re, ee = dot(a, n0), dot(a, n1), dot(a, n2)
    s1 = (rr - re - over_m(y1 * n0[0])) / (rr - 2.0 * re + ee - over_m(y1 * g))
    a0 = ((1.0 - s1) * a[0] + s1 * y1, (1.0 - s1) * a[1])
    a1 = (s1 * a[0], s1 * a[1])
    m0, m1, m2, m3 = apply(0, a0), apply(1, a0), apply(2, a0), apply(3, a0)
    l3, l4 = apply(3, a1), apply(4, a1)
    h = m0[0] + s1 * n1[0]
    g = h - (m1[0] + s1 * n2[0])
    y2 = solve(g)
    rr = dot(a0, m0) + 2.0 * dot(a1, m1) + s1 * dot(a1, n2)
    re = dot(a0, m1) + 2.0 * dot(a1, m2) + dot(a1, l3)
    ee = dot(a0, m2) + 2.0 * dot(a1, m3) + dot(a1, l4)
    s2 = (rr - re - over_m(y2 * h)) / (rr - 2.0 * re + ee - over_m(y2 * g))

    half = 0.5 * E3 * E3
    weights_r, weights_x = [], []
    for i in range(2):
        extra = s2 * y2 if i == 0 else 0.0
        weights_r.append((
            (1.0 - s2) * a0[i] + extra + half * s2 * a1[i],
            E3 * ((1.0 - s2) * a1[i] + s2 * a0[i]),
            half * s2 * a1[i],
        ))
        d0 = s1 * a[i] + s2 * a0[i]
        d1 = E3 * s2 * a1[i]
        weights_x.append((
            P0 * d0,
            P1 * d0 + (0.5 * P2) * d1,
            P2 * d0 + (0.5 * P1) * d1,
            P0 * d1,
            (0.5 * P1) * d1,
            (0.5 * P2) * d1,
        ))
    direct = coeffs - s1 * y1 - s2 * y2
    levels_r = (0, 3, 6)
    solid_r = [sum(w * TS[j] for w, j in zip(ws, levels_r)) for ws in weights_r]
    solid_x = [sum(w * TS[j] for j, w in enumerate(ws)) for ws in weights_x]

    odd = [(sub // step) % 2 == 1 for step in (1, 2, 4)]

    def each_over_m(values):
        for n, step in enumerate((1, 2, 4)):
            merged = []
            for u, v in zip(values[0::2], values[1::2]):
                stay, move = jnp.where(odd[n], v, u), jnp.where(odd[n], u, v)
                merged.append(stay + pltpu.roll(move, step, 0))
            values = merged
        return values[0]

    def tile(i):
        p, t = i // 4, i % 4
        rows = pl.ds(t * 8, 8)
        ff = fo[p, rows, :]
        base_x = guess[p, rows, :]
        parts_x, parts_r = [], []
        for q in range(8):
            b = t * 8 + q
            r = rm[p, b]
            dry = jnp.where(jnp.broadcast_to(ff[q : q + 1, :], (8, 128)) > 0.0, 0.0, r)
            us = [tm[j, p, b] for j in range(7)]
            vx = direct * r + solid_x[0] * dry
            for j in range(6):
                vx = vx + weights_x[0][j] * us[j]
            vr = solid_r[0] * dry
            for w, j in zip(weights_r[0], levels_r):
                vr = vr + w * us[j]
            parts_x.append(vx)
            parts_r.append(vr)
        base_x = base_x + each_over_m(parts_x)
        base_r = each_over_m(parts_r)
        dry = rs[p, rows, :]
        vs = [tr[j, p, rows, :] for j in range(7)]
        base_x = base_x + solid_x[1] * dry
        base_r = base_r + solid_r[1] * dry
        for j in range(6):
            base_x = base_x + weights_x[1][j] * vs[j]
        for w, j in zip(weights_r[1], levels_r):
            base_r = base_r + w * vs[j]
        out_x[p, rows, :] = base_x
        out_r[p, rows, :] = base_r

    def tiles(i, carry):
        for n in range(4):
            tile(4 * i + n)
        return carry

    lax.fori_loop(0, NA, tiles, 0)


def call(kernel, outs, scratch, limit, *args, aliases=None, cost=None):
    return pl.pallas_call(
        kernel,
        out_shape=tuple(jax.ShapeDtypeStruct(s, f32) for s in outs),
        in_specs=[VMEM] * len(args),
        out_specs=tuple([VMEM] * len(outs)),
        scratch_shapes=[pltpu.VMEM(s, f32) for s in scratch],
        input_output_aliases=aliases or {},
        cost_estimate=cost,
        compiler_params=pltpu.CompilerParams(vmem_limit_bytes=limit),
    )(*args)


def local(right_side, first_guess, recycled, heights, ground_codes):
    mib = 1 << 20
    long = pl.CostEstimate(flops=10**10, bytes_accessed=4 * 10**7, transcendentals=0)
    faces = ((XTILES, 8, 128), (XTILES, 8, 128), (YTILES, 8, 128), (YTILES, 8, 128))
    rm, *sends = call(
        vectors_kernel, ((NA * NB * K, 128), *faces), (), 4 * mib, recycled, cost=long
    )
    gnd, sxp, sxm, syp, sym = call(
        rest_kernel, ((4, 8, 128), *faces), (), 4 * mib,
        first_guess, right_side, heights, ground_codes, *sends,
        aliases={4: 1, 5: 2, 6: 3, 7: 4},
    )
    rm = rm.reshape(NA, NB, K, 128)

    def shift(value, axis, way):
        size = lax.axis_size(axis)
        pairs = [(i, i + way) for i in range(size) if 0 <= i + way < size]
        return lax.ppermute(value, axis, pairs)

    wide, flat = (PA, PB, 8, 128), (PA, QB, 128)
    fields = (wide, wide, wide, (7, NA, NB, 8, 128))
    small = ((2, 128, 128), (2, 128, 128), flat, flat)
    fxm, fxp = shift(sxp, "gx", 1), shift(sxm, "gx", -1)
    fym, fyp = shift(syp, "gy", 1), shift(sym, "gy", -1)
    state = call(inner_kernel, fields, small, 8 * mib, rm, gnd, cost=long)
    cp, cm = call(
        corner_kernel, ((CTILES, 8, 128), (CTILES, 8, 128)), (), 8 * mib, fxm, fxp
    )
    cym, cyp = shift(cp, "gy", 1), shift(cm, "gy", -1)
    state = call(
        strip_kernel, fields, small, 8 * mib, gnd, fxm, fxp, *state,
        aliases={3: 0, 4: 1, 5: 2, 6: 3}, cost=long,
    )
    pay, tr, rs, fo, _, _, _, tm = call(
        main_kernel,
        ((256, 2, 128), (7, NA, NB, 128), (NA, NB, 128), (NA, NB, 128), *fields),
        (flat, flat, flat, flat, (2, 128, 128), (2, 128, 128), (3, 8, 128)),
        8 * mib,
        rm, first_guess, right_side, gnd, fxm, fxp, fym, fyp, cym, cyp, *state,
        aliases={10: 4, 11: 5, 12: 6, 13: 7},
    )
    got = lax.all_to_all(pay, ("gx", "gy"), 0, 0)
    return call(
        tail_kernel,
        ((NA, NB, 128), (NA, NB, 128)),
        (),
        8 * mib,
        got, rm, first_guess, tm, tr, rs, fo,
    )


def solution(mesh):
    placed = (
        P("gx", "gy", None),
        P("gx", "gy", None),
        P(None, "gx", "gy", None),
        P("gx", "gy"),
        P("gx", "gy"),
    )
    return jax.shard_map(
        local,
        mesh=mesh,
        in_specs=placed,
        out_specs=(P("gx", "gy", None), P("gx", "gy", None)),
        check_vma=False,
    )
```
